256 devices in a mesh: member: 8 (over y, x_hi), space: 32 (over z, x_lo, core).
Axes of the slice: x: 4 (x_hi: 2, x_lo: 2; x = x_hi * 2 + x_lo), y: 4, z: 8, core: 2. Of those that a mesh axis runs over, the one named last changes fastest.
Arguments:
- zonal_wind: bfloat16 [48, 256, 256, 128], P('member', 'space'), may hold values from -6 to 6
- meridional_wind: bfloat16 [48, 256, 256, 128], P('member', 'space'), may hold values from -6 to 6
- heat_anomaly: bfloat16 [48, 256, 256, 128], P('member', 'space'), may hold values from -6 to 6
- moisture_anomaly: bfloat16 [48, 256, 256, 128], P('member', 'space'), may hold values from -6 to 6
- projection_scale: float32 [256, 256], P('space'), may hold values from 0.5 to 2
- balance_multiplier: float32 [256, 256], P('space'), may hold values from -4 to 4
- heat_on_curl_slope: float32 [128], replicated, may hold values from 0.3 to 1.5
- moisture_on_heat_slope: float32 [128], replicated, may hold values from 0.3 to 1.5
Outputs:
- covariance: float32 [32, 512, 512], P('space', 'member')
The draws below stay inside these ranges and needn't reach their ends.
All inputs are finite; a program needn't handle non-finite values.
Results may differ from the reference program's by a relative error of at most 0.0009.
Values may be sent and summed in bfloat16 or wider, within the bound.
No kernel may reach another device: no remote copies, remote signals or barrier semaphores. Data moves between devices by JAX's collectives and lax.ppermute only.
A program may use at most 128 MiB of HBM per device.

```python
import math
import jax
import jax.numpy as jnp
from jax import lax

HEIGHT_STEPS = 128
STATE = 512
STRIP_PARALLELS = 8
PATCH_MERIDIANS = 256
SAMPLE_COUNT = 48
BANDS = 32
GLOBE_PARALLELS = 256


def shard_levels(own_key, extent, shards, low, high):
    level, own = 1.0, jax.random.fold_in(own_key, 6)
    for position, shards_of in shards:
        heights = jnp.exp(jax.random.uniform(jax.random.fold_in(own, position), (shards_of,), jnp.float32, low / len(shards), high / len(shards)))
        level = level * jnp.repeat(heights, extent[position] // shards_of).reshape([-1 if axis == position else 1 for axis in range(len(extent))])
    return level


def gaussian(key, dims, spread, bound, pieces=(), held_as=jnp.bfloat16):
    result = jax.random.normal(key, dims, jnp.float32) * spread
    if len(pieces) > 0:
        result = shard_levels(key, dims, pieces, -0.22, 0.18) * result
    return jnp.clip(result, min=-bound, max=bound).astype(held_as)


def setup_inputs(seed: int = 0) -> dict:
    key_of = jax.random.split(jax.random.key(seed), 9)
    zonal_wind = gaussian(key_of[0], (SAMPLE_COUNT, GLOBE_PARALLELS, PATCH_MERIDIANS, HEIGHT_STEPS), 1.0, 6.0, ((0, 8), (1, 32)))
    meridional_wind = gaussian(key_of[1], (SAMPLE_COUNT, GLOBE_PARALLELS, PATCH_MERIDIANS, HEIGHT_STEPS), 1.0, 6.0, ((0, 8), (1, 32)))
    heat_anomaly = gaussian(key_of[2], (SAMPLE_COUNT, GLOBE_PARALLELS, PATCH_MERIDIANS, HEIGHT_STEPS), 1.0, 6.0, ((0, 8), (1, 32)))
    moisture_anomaly = gaussian(key_of[3], (SAMPLE_COUNT, GLOBE_PARALLELS, PATCH_MERIDIANS, HEIGHT_STEPS), 1.0, 6.0, ((0, 8), (1, 32)))
    projection_scale = jnp.clip(jnp.exp(math.log(2.0) - 1.3862944 * jax.random.uniform(key_of[4], (GLOBE_PARALLELS, PATCH_MERIDIANS), jnp.float32) ** shard_levels(key_of[4], (GLOBE_PARALLELS, PATCH_MERIDIANS), ((0, 32),), -0.2, 0.2)), 0.5, 2.0)
    balance_multiplier = gaussian(key_of[5], (GLOBE_PARALLELS, PATCH_MERIDIANS), 1.0, 4.0, ((0, 32),), jnp.float32)
    heat_on_curl_slope = jnp.clip(jax.random.uniform(key_of[6], (HEIGHT_STEPS,), jnp.float32, 0.3, 1.5), 0.3, 1.5)
    moisture_on_heat_slope = jnp.clip(jax.random.uniform(key_of[7], (HEIGHT_STEPS,), jnp.float32, 0.3, 1.5), 0.3, 1.5)
    return dict(zonal_wind=zonal_wind, meridional_wind=meridional_wind, heat_anomaly=heat_anomaly, moisture_anomaly=moisture_anomaly, projection_scale=projection_scale, balance_multiplier=balance_multiplier, heat_on_curl_slope=heat_on_curl_slope, moisture_on_heat_slope=moisture_on_heat_slope)


def lat_diff(padded):
    return (-padded[:, 4:] + 8.0 * padded[:, 3:-1] - 8.0 * padded[:, 1:-3] + padded[:, :-4]) / 12.0


def lon_diff(field):
    return (jnp.roll(field, -1, 2) - jnp.roll(field, 1, 2)) / 2.0


def derive_quantities(zonal_wind_bordered, meridional_wind_bordered, heat_anomaly, moisture_anomaly, projection_scale, balance_multiplier, heat_on_curl_slope, moisture_on_heat_slope):
    u_full = zonal_wind_bordered.astype(jnp.float32)
    v_full = meridional_wind_bordered.astype(jnp.float32)
    u_mid = u_full[:, 2:-2]
    v_mid = v_full[:, 2:-2]
    factor = projection_scale[None, :, :, None]
    wind_curl = factor * (lon_diff(v_mid) - lat_diff(u_full))
    wind_spreading = factor * (lon_diff(u_mid) + lat_diff(v_full))
    heat_residual = heat_anomaly.astype(jnp.float32) - heat_on_curl_slope * balance_multiplier[None, :, :, None] * wind_curl
    moisture_residual = moisture_anomaly.astype(jnp.float32) - moisture_on_heat_slope * heat_residual
    return jnp.concatenate([wind_curl, wind_spreading, heat_residual, moisture_residual], axis=3).astype(jnp.bfloat16)


def reference(zonal_wind, meridional_wind, heat_anomaly, moisture_anomaly, projection_scale, balance_multiplier, heat_on_curl_slope, moisture_on_heat_slope):
    u_pad = jnp.pad(zonal_wind, ((0, 0), (2, 2), (0, 0), (0, 0)))
    v_pad = jnp.pad(meridional_wind, ((0, 0), (2, 2), (0, 0), (0, 0)))

    def one_band(band):
        starting_parallel = (band * STRIP_PARALLELS).astype(jnp.int32)
        strip_zonal_wind = lax.dynamic_slice_in_dim(u_pad, starting_parallel, STRIP_PARALLELS + 4, 1)
        strip_meridional_wind = lax.dynamic_slice_in_dim(v_pad, starting_parallel, STRIP_PARALLELS + 4, 1)
        strip_heat = lax.dynamic_slice_in_dim(heat_anomaly, starting_parallel, STRIP_PARALLELS, 1)
        strip_moisture = lax.dynamic_slice_in_dim(moisture_anomaly, starting_parallel, STRIP_PARALLELS, 1)
        strip_scale_factor = lax.dynamic_slice_in_dim(projection_scale, starting_parallel, STRIP_PARALLELS, 0)
        strip_balance_factor = lax.dynamic_slice_in_dim(balance_multiplier, starting_parallel, STRIP_PARALLELS, 0)
        sample_vector = derive_quantities(strip_zonal_wind, strip_meridional_wind, strip_heat, strip_moisture, strip_scale_factor, strip_balance_factor, heat_on_curl_slope, moisture_on_heat_slope).astype(jnp.float32)
        ens_mean = jnp.sum(sample_vector, axis=0) / SAMPLE_COUNT
        anomaly = (sample_vector - ens_mean[None]).reshape(-1, STATE)
        moments = jnp.dot(anomaly.T, anomaly, preferred_element_type=jnp.float32, precision=lax.Precision.HIGHEST)
        return moments / ((SAMPLE_COUNT - 1) * STRIP_PARALLELS * PATCH_MERIDIANS)

    return lax.map(one_band, jnp.arange(BANDS, dtype=jnp.int32))
```

```python
import functools

import jax
import jax.numpy as jnp
from jax import lax
from jax.experimental import pallas as pl
from jax.experimental.pallas import tpu as pltpu
from jax.sharding import PartitionSpec as P

CHUNK = 32


def gram(a):
    return lax.dot_general(a, a, (((0,), (0,)), ((), ())), preferred_element_type=jnp.float32)


def rows_kernel(
    dims,
    late,
    u_hbm,
    v_hbm,
    h_hbm,
    q_hbm,
    halo_hbm,
    psi_ref,
    bal_ref,
    slopes_ref,
    g_ref,
    m_ref,
    u_ext,
    v_ext,
    h_buf,
    q_buf,
    d_buf,
    psi_b,
    sb_b,
    s_buf,
    sems,
):
    members, parallels, meridians, levels = dims
    core = lax.axis_index("space") % 2
    if late:
        n, own, own_from, own_to, halo_to, row_from = 2, 4, 4 * core, 2 * (1 - core), 4 * core, 6 * core
    else:
        n, own, own_from, own_to = parallels - 2, parallels, 0, 2 * core
        halo_to, row_from = parallels * (1 - core), 2 * (1 - core)

    copies = [
        pltpu.make_async_copy(halo_hbm.at[0], u_ext.at[:, pl.ds(halo_to, 2)], sems.at[0]),
        pltpu.make_async_copy(halo_hbm.at[1], v_ext.at[:, pl.ds(halo_to, 2)], sems.at[1]),
        pltpu.make_async_copy(u_hbm.at[:, pl.ds(own_from, own)], u_ext.at[:, pl.ds(own_to, own)], sems.at[2]),
        pltpu.make_async_copy(v_hbm.at[:, pl.ds(own_from, own)], v_ext.at[:, pl.ds(own_to, own)], sems.at[3]),
        pltpu.make_async_copy(h_hbm.at[:, pl.ds(row_from, n)], h_buf, sems.at[4]),
        pltpu.make_async_copy(q_hbm.at[:, pl.ds(row_from, n)], q_buf, sems.at[5]),
    ]
    for copy in copies:
        copy.start()

    row = lax.broadcasted_iota(jnp.int32, (meridians, meridians), 0)
    col = lax.broadcasted_iota(jnp.int32, (meridians, meridians), 1)
    east = (row + 1) % meridians == col
    west = (row + meridians - 1) % meridians == col
    stencil = jnp.where(east, 6.0, jnp.where(west, -6.0, 0.0)).astype(jnp.bfloat16)
    g_ref[...] = jnp.zeros_like(g_ref)
    slope_t = slopes_ref[0:1, :]
    slope_q = slopes_ref[1:2, :]

    for copy in copies:
        copy.wait()

    @pl.loop(0, n)
    def _(k):
        i = row_from + k
        psi_row = psi_ref[pl.ds(i, 1), :] * (1.0 / 12.0)
        bal_row = bal_ref[pl.ds(i, 1), :]
        psi_b[...] = jnp.transpose(jnp.broadcast_to(psi_row, (levels, meridians)))
        sb_b[...] = jnp.transpose(jnp.broadcast_to(bal_row, (levels, meridians))) * slope_t

        for m in range(members):
            winds = jnp.concatenate([v_ext[m, k + 2], u_ext[m, k + 2]], axis=1)
            d_buf[m] = jnp.dot(stencil, winds, preferred_element_type=jnp.float32)

        @pl.loop(0, meridians // CHUNK)
        def _(c):
            j = pl.multiple_of(c * CHUNK, CHUNK)
            at = pl.ds(j, CHUNK)
            psi = psi_b[at, :]
            sb = sb_b[at, :]
            total = [jnp.zeros((CHUNK, levels), jnp.float32) for _ in range(4)]
            for m in range(members):
                u = [u_ext[m, k + e, at, :].astype(jnp.float32) for e in (0, 1, 3, 4)]
                v = [v_ext[m, k + e, at, :].astype(jnp.float32) for e in (0, 1, 3, 4)]
                du = (u[2] - u[1]) * 8.0 - (u[3] - u[0])
                dv = (v[2] - v[1]) * 8.0 - (v[3] - v[0])
                curl = psi * (d_buf[m, at, 0:levels] - du)
                spread = psi * (d_buf[m, at, levels : 2 * levels] + dv)
                heat = h_buf[m, k, at, :].astype(jnp.float32) - sb * curl
                moist = q_buf[m, k, at, :].astype(jnp.float32) - slope_q * heat
                for f, x in enumerate((curl, spread, heat, moist)):
                    x = x.astype(jnp.bfloat16)
                    s_buf[m, at, f * levels : (f + 1) * levels] = x
                    total[f] = total[f] + x.astype(jnp.float32)
            for f in range(4):
                cut = slice(f * levels, (f + 1) * levels)
                mean = total[f] * (1.0 / members)
                m_ref[c, k, :, cut] = mean.astype(jnp.bfloat16)
                for m in range(members):
                    s_buf[m, at, cut] = (s_buf[m, at, cut].astype(jnp.float32) - mean).astype(jnp.bfloat16)

        g_ref[...] += gram(s_buf[...].reshape(members * meridians, 4 * levels))


def rows_call(dims, late, u, v, h, q, halo, psi, bal, slopes, peers):
    members, parallels, meridians, levels = dims
    n = 2 if late else parallels - 2
    width = 4 * levels
    any_spec = pl.BlockSpec(memory_space=pl.ANY)
    vmem_spec = pl.BlockSpec(memory_space=pltpu.VMEM)
    flops = 2 * n * members * meridians * (width * width + 2 * meridians * levels)
    return pl.pallas_call(
        functools.partial(rows_kernel, dims, late),
        name="late_rows" if late else "early_rows",
        out_shape=(
            jax.ShapeDtypeStruct((width, width), jnp.float32),
            jax.ShapeDtypeStruct((peers, n, CHUNK, width), jnp.bfloat16),
        ),
        in_specs=[any_spec] * 5 + [vmem_spec] * 3,
        out_specs=(vmem_spec, vmem_spec),
        scratch_shapes=[
            pltpu.VMEM((members, n + 4, meridians, levels), jnp.bfloat16),
            pltpu.VMEM((members, n + 4, meridians, levels), jnp.bfloat16),
            pltpu.VMEM((members, n, meridians, levels), jnp.bfloat16),
            pltpu.VMEM((members, n, meridians, levels), jnp.bfloat16),
            pltpu.VMEM((members, meridians, 2 * levels), jnp.float32),
            pltpu.VMEM((meridians, levels), jnp.float32),
            pltpu.VMEM((meridians, levels), jnp.float32),
            pltpu.VMEM((members, meridians, width), jnp.bfloat16),
            pltpu.SemaphoreType.DMA((6,)),
        ],
        compiler_params=pltpu.CompilerParams(vmem_limit_bytes=40 << 20),
        cost_estimate=pl.CostEstimate(flops=flops, bytes_accessed=16 << 20, transcendentals=0),
    )(u, v, h, q, halo, psi, bal, slopes)


def between_kernel(members, early_ref, late_ref, ge_ref, gl_ref, out_ref):
    total = ge_ref[...] + gl_ref[...]
    for part in (early_ref, late_ref):
        means = part[...].astype(jnp.float32)
        peers, n, chunk, width = means.shape
        overall = jnp.sum(means, axis=0, keepdims=True) * (1.0 / peers)
        apart = (means - overall).astype(jnp.bfloat16)
        total = total + gram(apart.reshape(peers * n * chunk, width)) * float(members)
    out_ref[...] = total


def between_call(members, early, late, ge, gl):
    vmem_spec = pl.BlockSpec(memory_space=pltpu.VMEM)
    return pl.pallas_call(
        functools.partial(between_kernel, members),
        name="between",
        out_shape=jax.ShapeDtypeStruct(ge.shape, jnp.float32),
        in_specs=[vmem_spec] * 4,
        out_specs=vmem_spec,
        compiler_params=pltpu.CompilerParams(vmem_limit_bytes=40 << 20),
        cost_estimate=pl.CostEstimate(flops=1 << 30, bytes_accessed=5 << 20, transcendentals=0),
    )(early, late, ge, gl)


def on_device(u, v, h, q, psi, bal, slope_t, slope_q):
    dims = u.shape
    members, parallels = dims[0], dims[1]
    count = lax.axis_size("space")
    peers = lax.axis_size("member")
    core = lax.axis_index("space") % 2
    slopes = jnp.stack([slope_t, slope_q])

    across = [(i, i + 1) for i in range(1, count - 1, 2)]
    across = across + [(b, a) for a, b in across]
    within = [(i, i + 1) for i in range(0, count, 2)]
    within = within + [(b, a) for a, b in within]

    def edge(start):
        return jnp.stack([lax.dynamic_slice_in_dim(x, start, 2, axis=1) for x in (u, v)])

    far = lax.ppermute(edge((parallels - 2) * core), "space", across)
    near = lax.ppermute(edge((parallels - 2) * (1 - core)), "space", within)

    ge, me = rows_call(dims, False, u, v, h, q, near, psi, bal, slopes, peers)
    me = lax.all_to_all(me, "member", 0, 0, tiled=True)
    gl, ml = rows_call(dims, True, u, v, h, q, far, psi, bal, slopes, peers)
    ml = lax.all_to_all(ml, "member", 0, 0, tiled=True)
    total = between_call(members, me, ml, ge, gl)
    width = total.shape[0]
    parts = lax.all_to_all(total.reshape(peers, width // peers, width), "member", 0, 0, tiled=True)
    scale = 1.0 / ((members * peers - 1) * parallels * dims[2])
    return (jnp.sum(parts, axis=0) * scale)[None]


def solution(mesh):
    placed = (P("member", "space", None, None),) * 4 + (P("space", None),) * 2 + (P(), P())
    return jax.shard_map(
        on_device, mesh=mesh, in_specs=placed, out_specs=P("space", "member", None), check_vma=False
    )
```

```python
import functools

import jax
import jax.numpy as jnp
from jax import lax
from jax.experimental import pallas as pl
from jax.experimental.pallas import tpu as pltpu
from jax.sharding import PartitionSpec as P

ANY = pl.BlockSpec(memory_space=pl.ANY)
VMEM = pl.BlockSpec(memory_space=pltpu.VMEM)
HBM = pl.BlockSpec(memory_space=pltpu.HBM)
SIDE = 2
EDGE = 2


def params(mebibytes):
    return pltpu.CompilerParams(vmem_limit_bytes=mebibytes << 20)


def cost(flops, moved):
    return pl.CostEstimate(flops=flops, bytes_accessed=moved, transcendentals=0)


def gram(a):
    return lax.dot_general(a, a, (((0,), (0,)), ((), ())), preferred_element_type=jnp.float32)


def core_index():
    return lax.axis_index("space") % 2


def run(copies):
    for copy in copies:
        copy.start()


def finish(copies):
    for copy in copies:
        copy.wait()


def edges_kernel(parallels, u_hbm, v_hbm, far_ref, near_ref, sums_ref, sems):
    core = core_index()
    far_at = pl.ds((parallels - EDGE) * core, EDGE)
    near_at = pl.ds((parallels - EDGE) * (1 - core), EDGE)
    far = [pltpu.make_async_copy(x.at[:, far_at], far_ref.at[f], sems.at[f]) for f, x in enumerate((u_hbm, v_hbm))]
    near = [pltpu.make_async_copy(x.at[:, near_at], near_ref.at[f], sems.at[2 + f]) for f, x in enumerate((u_hbm, v_hbm))]
    run(far + near)
    for f in range(2):
        far[f].wait()
        for r in range(EDGE):
            total = far_ref[f, 0, r].astype(jnp.float32)
            for m in range(1, far_ref.shape[1]):
                total = total + far_ref[f, m, r].astype(jnp.float32)
            sums_ref[f, r] = total.astype(jnp.bfloat16)
    finish(near)


def edges_call(u, v):
    members, parallels, meridians, levels = u.shape
    edge = jax.ShapeDtypeStruct((2, members, EDGE, meridians, levels), u.dtype)
    return pl.pallas_call(
        functools.partial(edges_kernel, parallels),
        name="edges",
        out_shape=(edge, edge, jax.ShapeDtypeStruct((2, EDGE, meridians, levels), u.dtype)),
        in_specs=[HBM, HBM],
        out_specs=(VMEM, VMEM, VMEM),
        scratch_shapes=[pltpu.SemaphoreType.DMA((4,))],
        compiler_params=params(8),
        cost_estimate=cost(1 << 20, 6 << 20),
    )(u, v)


def spread_over(ref, rows_at, psi_b, sb_b, psi_ref, bal_ref, slope_t):
    meridians, levels = psi_b.shape
    psi_row = psi_ref[pl.ds(rows_at, 1), :] * (1.0 / 12.0)
    bal_row = bal_ref[pl.ds(rows_at, 1), :]
    psi_b[...] = jnp.transpose(jnp.broadcast_to(psi_row, (levels, meridians)))
    sb_b[...] = jnp.transpose(jnp.broadcast_to(bal_row, (levels, meridians))) * slope_t


def lat_diff(rows):
    return (rows[2] - rows[1]) * 8.0 - (rows[3] - rows[0])


def compute_rows(n, row_from, u_ext, v_ext, h_buf, q_buf, psi_ref, bal_ref, slopes_ref, d_buf, psi_b, sb_b, s_buf, g_ref, m_scr, mean_ref, chunk):
    members, _, meridians, levels = u_ext.shape
    row = lax.broadcasted_iota(jnp.int32, (meridians, meridians), 0)
    col = lax.broadcasted_iota(jnp.int32, (meridians, meridians), 1)
    east = (row + 1) % meridians == col
    west = (row + meridians - 1) % meridians == col
    stencil = jnp.where(east, 6.0, jnp.where(west, -6.0, 0.0)).astype(jnp.bfloat16)
    slope_t = slopes_ref[0:1, :]
    slope_q = slopes_ref[1:2, :]

    @pl.loop(0, n)
    def _(k):
        spread_over(None, row_from + k, psi_b, sb_b, psi_ref, bal_ref, slope_t)
        for m in range(members):
            winds = jnp.concatenate([v_ext[m, k + 2], u_ext[m, k + 2]], axis=1)
            d_buf[m] = jnp.dot(stencil, winds, preferred_element_type=jnp.float32)

        @pl.loop(0, meridians // chunk)
        def _(c):
            at = pl.ds(pl.multiple_of(c * chunk, chunk), chunk)
            psi = psi_b[at, :]
            sb = sb_b[at, :]
            total = [jnp.zeros((chunk, levels), jnp.float32) for _ in range(4)]
            for m in range(members):
                du = lat_diff([u_ext[m, k + e, at, :].astype(jnp.float32) for e in (0, 1, 3, 4)])
                dv = lat_diff([v_ext[m, k + e, at, :].astype(jnp.float32) for e in (0, 1, 3, 4)])
                curl = psi * (d_buf[m, at, 0:levels] - du)
                spread = psi * (d_buf[m, at, levels : 2 * levels] + dv)
                heat = h_buf[m, k, at, :].astype(jnp.float32) - sb * curl
                moist = q_buf[m, k, at, :].astype(jnp.float32) - slope_q * heat
                for f, x in enumerate((curl, spread, heat, moist)):
                    cut = slice(f * levels, (f + 1) * levels)
                    x = x.astype(jnp.bfloat16)
                    if mean_ref is None:
                        s_buf[m, at, cut] = x
                        total[f] = total[f] + x.astype(jnp.float32)
                    else:
                        mean = mean_ref[c, k, :, cut].astype(jnp.float32)
                        s_buf[m, at, cut] = (x.astype(jnp.float32) - mean).astype(jnp.bfloat16)
            if mean_ref is None:
                for f in range(4):
                    cut = slice(f * levels, (f + 1) * levels)
                    mean = total[f] * (1.0 / members)
                    m_scr[c, k, :, cut] = mean.astype(jnp.bfloat16)
                    for m in range(members):
                        s_buf[m, at, cut] = (s_buf[m, at, cut].astype(jnp.float32) - mean).astype(jnp.bfloat16)

        g_ref[...] += gram(s_buf[...].reshape(members * meridians, 4 * levels))


def scatter_means(m_scr, outs, first, sem, groups):
    y = lax.axis_index("member") // SIDE
    n = m_scr.shape[1]
    return [
        pltpu.make_async_copy(
            m_scr.at[pl.ds(SIDE * lax.rem(y + r, groups), SIDE)], out.at[:, pl.ds(first, n)], sem.at[r]
        )
        for r, out in enumerate(outs)
    ]


def inner_kernel(chunk, u_hbm, v_hbm, h_hbm, q_hbm, psi_ref, bal_ref, slopes_ref, g_ref, *rest):
    outs, (u_ext, v_ext, h_buf, q_buf, d_buf, psi_b, sb_b, s_buf, m_scr, sems, out_sems) = rest[:-11], rest[-11:]
    n = h_buf.shape[1]
    copies = [
        pltpu.make_async_copy(u_hbm, u_ext, sems.at[0]),
        pltpu.make_async_copy(v_hbm, v_ext, sems.at[1]),
        pltpu.make_async_copy(h_hbm.at[:, pl.ds(EDGE, n)], h_buf, sems.at[2]),
        pltpu.make_async_copy(q_hbm.at[:, pl.ds(EDGE, n)], q_buf, sems.at[3]),
    ]
    run(copies)
    g_ref[...] = jnp.zeros_like(g_ref)
    finish(copies)
    compute_rows(n, EDGE, u_ext, v_ext, h_buf, q_buf, psi_ref, bal_ref, slopes_ref, d_buf, psi_b, sb_b, s_buf, g_ref, m_scr, None, chunk)
    sends = scatter_means(m_scr, outs, 0, out_sems, len(outs))
    run(sends)
    finish(sends)


def edge_copies(side, u_hbm, v_hbm, h_hbm, q_hbm, halo, u_ext, v_ext, h_buf, q_buf, sems):
    parallels = u_hbm.shape[1]
    own = u_ext.shape[1] - EDGE
    own_from = pl.ds((parallels - own) * side, own)
    own_to = pl.ds(EDGE * (1 - side), own)
    halo_to = pl.ds(own * side, EDGE)
    row_from = pl.ds((parallels - EDGE) * side, EDGE)
    copies = [
        pltpu.make_async_copy(u_hbm.at[:, own_from], u_ext.at[:, own_to], sems.at[0]),
        pltpu.make_async_copy(v_hbm.at[:, own_from], v_ext.at[:, own_to], sems.at[1]),
        pltpu.make_async_copy(h_hbm.at[:, row_from], h_buf, sems.at[2]),
        pltpu.make_async_copy(q_hbm.at[:, row_from], q_buf, sems.at[3]),
    ]
    if halo is not None:
        copies.append(pltpu.make_async_copy(halo.at[0], u_ext.at[:, halo_to], sems.at[4]))
        copies.append(pltpu.make_async_copy(halo.at[1], v_ext.at[:, halo_to], sems.at[5]))
    return copies


def near_kernel(chunk, u_hbm, v_hbm, h_hbm, q_hbm, near_hbm, far_sums_ref, psi_ref, bal_ref, slopes_ref, g_in_ref, g_ref, late_ref, *rest):
    outs, scratch = rest[:-14], rest[-14:]
    u_ext, v_ext, h_buf, q_buf, d_buf, psi_b, sb_b, s_buf, m_scr, u_sum, v_sum, sems, late_sems, out_sems = scratch
    members, parallels, meridians, levels = u_hbm.shape
    core = core_index()
    side = 1 - core
    copies = edge_copies(side, u_hbm, v_hbm, h_hbm, q_hbm, near_hbm, u_ext, v_ext, h_buf, q_buf, sems)
    run(copies)
    g_ref[...] = g_in_ref[...]
    finish(copies)
    compute_rows(EDGE, (parallels - EDGE) * side, u_ext, v_ext, h_buf, q_buf, psi_ref, bal_ref, slopes_ref, d_buf, psi_b, sb_b, s_buf, g_ref, m_scr, None, chunk)
    near_sends = scatter_means(m_scr, outs, 0, out_sems, len(outs))
    run(near_sends)

    copies = edge_copies(core, u_hbm, v_hbm, h_hbm, q_hbm, None, u_ext, v_ext, h_buf, q_buf, late_sems)
    run(copies)
    own = u_ext.shape[1] - EDGE
    finish(copies)
    for f, (ext, total) in enumerate(((u_ext, u_sum), (v_ext, v_sum))):
        for r in range(EDGE):
            total[own * core + r] = far_sums_ref[f, r].astype(jnp.float32)
        for r in range(own):
            e = EDGE * (1 - core) + r
            total[e] = sum(ext[m, e].astype(jnp.float32) for m in range(members))
    for k in range(EDGE):
        spread_over(None, (parallels - EDGE) * core + k, psi_b, sb_b, psi_ref, bal_ref, slopes_ref[0:1, :])
        du = lat_diff([u_sum[k + e] for e in (0, 1, 3, 4)])
        dv = lat_diff([v_sum[k + e] for e in (0, 1, 3, 4)])
        east = [(pltpu.roll(x[k + 2], meridians - 1, 0) - pltpu.roll(x[k + 2], 1, 0)) * 6.0 for x in (v_sum, u_sum)]
        curl = psi_b[...] * (east[0] - du)
        spread = psi_b[...] * (east[1] + dv)
        heat = sum(h_buf[m, k].astype(jnp.float32) for m in range(members)) - sb_b[...] * curl
        moist = sum(q_buf[m, k].astype(jnp.float32) for m in range(members)) - slopes_ref[1:2, :] * heat
        for f, x in enumerate((curl, spread, heat, moist)):
            mean = (x * (1.0 / members)).astype(jnp.bfloat16)
            late_ref[:, k, :, f * levels : (f + 1) * levels] = mean.reshape(meridians // chunk, chunk, levels)
    late_sends = scatter_means(late_ref, outs, EDGE, late_sems, len(outs))
    run(late_sends)
    finish(near_sends + late_sends)


def far_kernel(chunk, u_hbm, v_hbm, h_hbm, q_hbm, far_hbm, late_ref, psi_ref, bal_ref, slopes_ref, g_in_ref, mine_ref, theirs_ref, g_ref, u_ext, v_ext, h_buf, q_buf, d_buf, psi_b, sb_b, s_buf, sems):
    members, parallels, meridians, levels = u_hbm.shape
    core = core_index()
    copies = edge_copies(core, u_hbm, v_hbm, h_hbm, q_hbm, far_hbm, u_ext, v_ext, h_buf, q_buf, sems)
    run(copies)
    groups = lax.axis_size("member") // SIDE
    apart = (mine_ref[...].astype(jnp.float32) - theirs_ref[...].astype(jnp.float32)).astype(jnp.bfloat16)
    apart = apart.reshape(-1, 4 * levels)
    g_ref[...] = g_in_ref[...] + gram(apart) * (members * groups / 2.0)
    finish(copies)
    compute_rows(EDGE, (parallels - EDGE) * core, u_ext, v_ext, h_buf, q_buf, psi_ref, bal_ref, slopes_ref, d_buf, psi_b, sb_b, s_buf, g_ref, None, late_ref, chunk)


def row_scratch(dims, n, ext):
    members, _, meridians, levels = dims
    return [
        pltpu.VMEM((members, ext, meridians, levels), jnp.bfloat16),
        pltpu.VMEM((members, ext, meridians, levels), jnp.bfloat16),
        pltpu.VMEM((members, n, meridians, levels), jnp.bfloat16),
        pltpu.VMEM((members, n, meridians, levels), jnp.bfloat16),
        pltpu.VMEM((members, meridians, 2 * levels), jnp.float32),
        pltpu.VMEM((meridians, levels), jnp.float32),
        pltpu.VMEM((meridians, levels), jnp.float32),
        pltpu.VMEM((members, meridians, 4 * levels), jnp.bfloat16),
    ]


def row_cost(dims, n):
    members, _, meridians, levels = dims
    return cost(4 * n * members * meridians * 16 * levels * levels, 8 << 20)


def between_kernel(members, g_in_ref, *rest):
    parts, (g_ref, mine_ref, theirs_ref) = rest[:-3], rest[-3:]
    side = lax.axis_index("member") % SIDE
    groups = len(parts) // 2
    total = g_in_ref[...]
    first = 0
    for part in (parts[:groups], parts[groups:]):
        _, n, chunk, width = part[0].shape
        overall = sum(p[...].astype(jnp.float32) for p in part) * (1.0 / groups)
        apart = [(p[...].astype(jnp.float32) - overall).astype(jnp.bfloat16).reshape(-1, width) for p in part]
        total = total + gram(jnp.concatenate(apart, axis=0)) * float(members)
        overall = overall.astype(jnp.bfloat16)
        low = side == 0
        mine_ref[first : first + n] = jnp.where(low, overall[0], overall[1])
        theirs_ref[first : first + n] = jnp.where(low, overall[1], overall[0])
        first += n
    g_ref[...] = total


def on_device(u, v, h, q, psi, bal, slope_t, slope_q):
    dims = members, parallels, meridians, levels = u.shape
    width = 4 * levels
    count = lax.axis_size("space")
    peers = lax.axis_size("member")
    groups = peers // SIDE
    chunk = meridians // peers
    inner = parallels - 2 * EDGE
    slopes = jnp.stack([slope_t, slope_q])

    across = [(i, i + 1) for i in range(1, count - 1, 2)]
    across = across + [(b, a) for a, b in across]
    within = [(i, i + 1) for i in range(0, count, 2)]
    within = within + [(b, a) for a, b in within]

    def along_y(r):
        return [(y * SIDE + x, (y + r) % groups * SIDE + x) for y in range(groups) for x in range(SIDE)]

    along_x = [(y * SIDE + x, y * SIDE + 1 - x) for y in range(groups) for x in range(SIDE)]

    far_edge, near_edge, far_sums = edges_call(u, v)
    far_sums = lax.ppermute(far_sums, "space", across)
    far = lax.ppermute(far_edge, "space", across)
    near = lax.ppermute(near_edge, "space", within)

    g_shape = jax.ShapeDtypeStruct((width, width), jnp.float32)
    handed = lambda n: (jax.ShapeDtypeStruct((SIDE, n, chunk, width), jnp.bfloat16),) * groups

    g, *inner_means = pl.pallas_call(
        functools.partial(inner_kernel, chunk),
        name="inner_rows",
        out_shape=(g_shape,) + handed(inner),
        in_specs=[HBM] * 4 + [VMEM] * 3,
        out_specs=(VMEM,) + (ANY,) * groups,
        scratch_shapes=row_scratch(dims, inner, parallels)
        + [pltpu.VMEM((peers, inner, chunk, width), jnp.bfloat16), pltpu.SemaphoreType.DMA((4,)), pltpu.SemaphoreType.DMA((groups,))],
        compiler_params=params(20),
        cost_estimate=row_cost(dims, inner),
    )(u, v, h, q, psi, bal, slopes)
    inner_means = [x if r == 0 else lax.ppermute(x, "member", along_y(r)) for r, x in enumerate(inner_means)]

    sum_shape = (2 * EDGE + EDGE, meridians, levels)
    g, late, *edge_means = pl.pallas_call(
        functools.partial(near_kernel, chunk),
        name="near_rows",
        out_shape=(g_shape, jax.ShapeDtypeStruct((peers, EDGE, chunk, width), jnp.bfloat16)) + handed(2 * EDGE),
        in_specs=[HBM] * 4 + [ANY] + [VMEM] * 5,
        out_specs=(VMEM, VMEM) + (ANY,) * groups,
        scratch_shapes=row_scratch(dims, EDGE, 3 * EDGE)
        + [pltpu.VMEM((peers, EDGE, chunk, width), jnp.bfloat16), pltpu.VMEM(sum_shape, jnp.float32), pltpu.VMEM(sum_shape, jnp.float32)]
        + [pltpu.SemaphoreType.DMA((6,)), pltpu.SemaphoreType.DMA((4,)), pltpu.SemaphoreType.DMA((groups,))],
        compiler_params=params(18),
        cost_estimate=row_cost(dims, EDGE),
    )(u, v, h, q, near, far_sums, psi, bal, slopes, g)
    edge_means = [x if r == 0 else lax.ppermute(x, "member", along_y(r)) for r, x in enumerate(edge_means)]

    half = jax.ShapeDtypeStruct((parallels, chunk, width), jnp.bfloat16)
    g, mine, theirs = pl.pallas_call(
        functools.partial(between_kernel, members),
        name="between",
        out_shape=(g_shape, half, half),
        in_specs=[VMEM] * (1 + 2 * groups),
        out_specs=(VMEM, VMEM, VMEM),
        compiler_params=params(16),
        cost_estimate=cost(1 << 30, 5 << 20),
    )(g, *inner_means, *edge_means)
    theirs = lax.ppermute(theirs, "member", along_x)

    g = pl.pallas_call(
        functools.partial(far_kernel, chunk),
        name="far_rows",
        out_shape=g_shape,
        in_specs=[ANY] * 5 + [VMEM] * 7,
        out_specs=VMEM,
        scratch_shapes=row_scratch(dims, EDGE, 3 * EDGE) + [pltpu.SemaphoreType.DMA((6,))],
        compiler_params=params(18),
        cost_estimate=row_cost(dims, EDGE),
    )(u, v, h, q, far, late, psi, bal, slopes, g, mine, theirs)

    parts = lax.all_to_all(g.reshape(peers, width // peers, width), "member", 0, 0, tiled=True)
    scale = 1.0 / ((members * peers - 1) * parallels * meridians)
    return (jnp.sum(parts, axis=0) * scale)[None]


def solution(mesh):
    placed = (P("member", "space", None, None),) * 4 + (P("space", None),) * 2 + (P(), P())
    return jax.shard_map(
        on_device, mesh=mesh, in_specs=placed, out_specs=P("space", "member", None), check_vma=False
    )
```

```python
import functools

import jax
import jax.numpy as jnp
from jax import lax
from jax.experimental import pallas as pl
from jax.experimental.pallas import tpu as pltpu
from jax.sharding import PartitionSpec as P

ANY = pl.BlockSpec(memory_space=pl.ANY)
VMEM = pl.BlockSpec(memory_space=pltpu.VMEM)
SIDE = 2
EDGE = 2


def params(mebibytes):
    return pltpu.CompilerParams(vmem_limit_bytes=mebibytes << 20)


def in_hbm(x):
    return pltpu.with_memory_space_constraint(x, pltpu.HBM)


def cost(flops, moved):
    return pl.CostEstimate(flops=flops, bytes_accessed=moved, transcendentals=0)


def gram(a, b):
    return lax.dot_general(a, b, (((0,), (0,)), ((), ())), preferred_element_type=jnp.float32)


def core_index():
    return lax.axis_index("space") % 2


def run(copies):
    for copy in copies:
        copy.start()


def finish(copies):
    for copy in copies:
        copy.wait()


def edges_kernel(parallels, u_hbm, v_hbm, far_ref, near_ref, sums_ref, sems):
    core = core_index()
    far_at = pl.ds((parallels - EDGE) * core, EDGE)
    near_at = pl.ds((parallels - EDGE) * (1 - core), EDGE)
    far = [pltpu.make_async_copy(x.at[:, far_at], far_ref.at[f], sems.at[f]) for f, x in enumerate((u_hbm, v_hbm))]
    near = [pltpu.make_async_copy(x.at[:, near_at], near_ref.at[f], sems.at[2 + f]) for f, x in enumerate((u_hbm, v_hbm))]
    run(far + near)
    for f in range(2):
        far[f].wait()
        for r in range(EDGE):
            total = far_ref[f, 0, r].astype(jnp.float32)
            for m in range(1, far_ref.shape[1]):
                total = total + far_ref[f, m, r].astype(jnp.float32)
            sums_ref[f, r] = total.astype(jnp.bfloat16)
    finish(near)


def edges_call(u, v):
    members, parallels, meridians, levels = u.shape
    edge = jax.ShapeDtypeStruct((2, members, EDGE, meridians, levels), u.dtype)
    return pl.pallas_call(
        functools.partial(edges_kernel, parallels),
        name="edges",
        out_shape=(edge, edge, jax.ShapeDtypeStruct((2, EDGE, meridians, levels), u.dtype)),
        in_specs=[ANY, ANY],
        out_specs=(VMEM, VMEM, VMEM),
        scratch_shapes=[pltpu.SemaphoreType.DMA((4,))],
        compiler_params=params(50),
        cost_estimate=cost(1 << 20, 6 << 20),
    )(u, v)


def spread_over(at, psi_ref, bal_ref, slope_t, levels):
    shape = (levels, psi_ref.shape[1])
    psi = jnp.transpose(jnp.broadcast_to(psi_ref[pl.ds(at, 1), :] * (1.0 / 12.0), shape))
    balance = jnp.transpose(jnp.broadcast_to(bal_ref[pl.ds(at, 1), :], shape))
    return psi, balance * slope_t


def lat_diff(rows):
    return (rows[2] - rows[1]) * 8.0 - (rows[3] - rows[0])


def add_gram(g_ref, a):
    half = a.shape[1] // 2
    g_ref[0:half] += gram(a[:, :half], a)
    g_ref[half:, half:] += gram(a[:, half:], a[:, half:])


def compute_rows(n, row_from, winds, scalars, psi_ref, bal_ref, slopes_ref, work, g_ref, m_ref, known, chunk, ready=lambda: None):
    u_ext, v_ext = winds
    h_buf, q_buf = scalars
    d_bufs, psi_bs, sb_bs, s_bufs = work[0:2], work[2:4], work[4:6], work[6:8]
    members, _, meridians, levels = u_ext.shape
    row = lax.broadcasted_iota(jnp.int32, (meridians, meridians), 0)
    col = lax.broadcasted_iota(jnp.int32, (meridians, meridians), 1)
    east = (row + 1) % meridians == col
    west = (row + meridians - 1) % meridians == col
    stencil = jnp.where(east, 6.0, jnp.where(west, -6.0, 0.0)).astype(jnp.bfloat16)
    slope_t = slopes_ref[0:1, :]
    slope_q = slopes_ref[1:2, :]
    half = meridians // 2
    cuts = [slice(f * levels, (f + 1) * levels) for f in range(4)]

    def prepare(k):
        b = k % 2
        psi_bs[b][...], sb_bs[b][...] = spread_over(row_from + k, psi_ref, bal_ref, slope_t, levels)
        for m in range(members):
            both = jnp.concatenate([v_ext[m, k + EDGE], u_ext[m, k + EDGE]], axis=1)
            d_bufs[b][m] = jnp.dot(stencil, both, preferred_element_type=jnp.float32)

    def derive(k, part):
        b = k % 2
        s_buf = s_bufs[part]
        for start in range(0, half, chunk):
            c = (part * half + start) // chunk
            at = slice(c * chunk, (c + 1) * chunk)
            to = slice(start, start + chunk)
            psi = psi_bs[b][at, :]
            sb = sb_bs[b][at, :]
            total = [None] * 4
            for m in range(members):
                du = lat_diff([u_ext[m, k + e, at, :].astype(jnp.float32) for e in (0, 1, 3, 4)])
                dv = lat_diff([v_ext[m, k + e, at, :].astype(jnp.float32) for e in (0, 1, 3, 4)])
                curl = psi * (d_bufs[b][m, at, 0:levels] - du)
                spread = psi * (d_bufs[b][m, at, levels : 2 * levels] + dv)
                heat = h_buf[m, k, at, :].astype(jnp.float32) - sb * curl
                moist = q_buf[m, k, at, :].astype(jnp.float32) - slope_q * heat
                for f, x in enumerate((curl, spread, heat, moist)):
                    x = x.astype(jnp.bfloat16)
                    if known:
                        mean = m_ref[c, k, :, cuts[f]].astype(jnp.float32)
                        s_buf[m, to, cuts[f]] = (x.astype(jnp.float32) - mean).astype(jnp.bfloat16)
                    else:
                        s_buf[m, to, cuts[f]] = x
                        x = x.astype(jnp.float32)
                        total[f] = x if m == 0 else total[f] + x
            if not known:
                for f, cut in enumerate(cuts):
                    mean = total[f] * (1.0 / members)
                    m_ref[c, k, :, cut] = mean.astype(jnp.bfloat16)
                    for m in range(members):
                        s_buf[m, to, cut] = (s_buf[m, to, cut].astype(jnp.float32) - mean).astype(jnp.bfloat16)

    def take(part):
        s_buf = s_bufs[part]
        add_gram(g_ref, s_buf[...].reshape(-1, s_buf.shape[2]))

    prepare(0)
    ready()
    for k in range(n):
        derive(k, 0)
        if k > 0:
            take(1)
        if k + 1 < n:
            prepare(k + 1)
        derive(k, 1)
        take(0)
    take(1)


def scatter_means(m_scr, outs, first, sem, groups):
    y = lax.axis_index("member") // SIDE
    n = m_scr.shape[1]
    return [
        pltpu.make_async_copy(
            m_scr.at[pl.ds(SIDE * lax.rem(y + r, groups), SIDE)], out.at[:, pl.ds(first, n)], sem.at[r]
        )
        for r, out in enumerate(outs)
    ]


def inner_kernel(chunk, u_hbm, v_hbm, h_hbm, q_hbm, psi_ref, bal_ref, slopes_ref, g_ref, *rest):
    outs, scratch = rest[:-15], rest[-15:]
    u_ext, v_ext, h_buf, q_buf = scratch[:4]
    work = scratch[4:12]
    m_scr, sems, out_sems = scratch[12:]
    n = m_scr.shape[1]
    inner = pl.ds(EDGE, n)
    pairs = ((u_hbm, u_ext), (v_hbm, v_ext), (h_hbm.at[:, inner], h_buf), (q_hbm.at[:, inner], q_buf))
    copies = [pltpu.make_async_copy(x, y, sems.at[i]) for i, (x, y) in enumerate(pairs)]
    run(copies)
    g_ref[...] = jnp.zeros_like(g_ref)
    finish(copies[:2])
    compute_rows(n, EDGE, (u_ext, v_ext), (h_buf, q_buf), psi_ref, bal_ref, slopes_ref, work, g_ref, m_scr, False, chunk, lambda: finish(copies[2:]))
    sends = scatter_means(m_scr, outs, 0, out_sems, len(outs))
    run(sends)
    finish(sends)


def edge_copies(side, u_hbm, v_hbm, h_hbm, q_hbm, halo, u_ext, v_ext, h_buf, q_buf, sems):
    parallels = u_hbm.shape[1]
    own = u_ext.shape[1] - EDGE
    own_from = pl.ds((parallels - own) * side, own)
    own_to = pl.ds(EDGE * (1 - side), own)
    halo_to = pl.ds(own * side, EDGE)
    row_from = pl.ds((parallels - EDGE) * side, EDGE)
    copies = [
        pltpu.make_async_copy(u_hbm.at[:, own_from], u_ext.at[:, own_to], sems.at[0]),
        pltpu.make_async_copy(v_hbm.at[:, own_from], v_ext.at[:, own_to], sems.at[1]),
        pltpu.make_async_copy(h_hbm.at[:, row_from], h_buf, sems.at[2]),
        pltpu.make_async_copy(q_hbm.at[:, row_from], q_buf, sems.at[3]),
    ]
    if halo is not None:
        copies.append(pltpu.make_async_copy(halo.at[0], u_ext.at[:, halo_to], sems.at[4]))
        copies.append(pltpu.make_async_copy(halo.at[1], v_ext.at[:, halo_to], sems.at[5]))
    return copies


def near_kernel(chunk, u_hbm, v_hbm, h_hbm, q_hbm, near_hbm, far_sums_ref, psi_ref, bal_ref, slopes_ref, g_in_ref, g_ref, late_ref, *rest):
    outs, scratch = rest[:-22], rest[-22:]
    u_ext, v_ext, h_buf, q_buf = scratch[:4]
    work = scratch[4:12]
    m_scr, u_sum, v_sum, sems, out_sems, late_sems = scratch[12:18]
    members, parallels, meridians, levels = u_hbm.shape
    side = 1 - core_index()
    copies = edge_copies(side, u_hbm, v_hbm, h_hbm, q_hbm, near_hbm, u_ext, v_ext, h_buf, q_buf, sems)
    run(copies)
    copies_far = edge_copies(1 - side, u_hbm, v_hbm, h_hbm, q_hbm, None, *scratch[18:22], late_sems)
    run(copies_far)
    g_ref[...] = g_in_ref[...]
    finish(copies)
    compute_rows(EDGE, (parallels - EDGE) * side, (u_ext, v_ext), (h_buf, q_buf), psi_ref, bal_ref, slopes_ref, work, g_ref, m_scr, False, chunk)
    sends = scatter_means(m_scr, outs, 0, out_sems, len(outs))
    run(sends)

    finish(copies_far)
    u_ext, v_ext, h_buf, q_buf = scratch[18:22]
    core = core_index()
    own = 2 * EDGE
    row_from = (parallels - EDGE) * core
    for f, (ext, total) in enumerate(((u_ext, u_sum), (v_ext, v_sum))):
        for r in range(EDGE):
            total[own * core + r] = far_sums_ref[f, r].astype(jnp.float32)
        for r in range(own):
            total[EDGE * (1 - core) + r] = sum(ext[m, EDGE * (1 - core) + r].astype(jnp.float32) for m in range(members))
    for k in range(EDGE):
        work[2][...], work[4][...] = spread_over(row_from + k, psi_ref, bal_ref, slopes_ref[0:1, :], levels)
        for c in range(meridians // chunk):
            at = slice(c * chunk, (c + 1) * chunk)
            du = lat_diff([u_sum[k + e, at] for e in (0, 1, 3, 4)])
            dv = lat_diff([v_sum[k + e, at] for e in (0, 1, 3, 4)])
            work[0][0, at, 0:levels] = du
            work[0][0, at, levels : 2 * levels] = dv
        east = [(pltpu.roll(x[k + EDGE], meridians - 1, 0) - pltpu.roll(x[k + EDGE], 1, 0)) * 6.0 for x in (v_sum, u_sum)]
        work[1][0, :, 0:levels] = east[0]
        work[1][0, :, levels : 2 * levels] = east[1]
        for c in range(meridians // chunk):
            at = slice(c * chunk, (c + 1) * chunk)
            psi = work[2][at]
            curl = psi * (work[1][0, at, 0:levels] - work[0][0, at, 0:levels])
            spread = psi * (work[1][0, at, levels : 2 * levels] + work[0][0, at, levels : 2 * levels])
            heat = sum(h_buf[m, k, at].astype(jnp.float32) for m in range(members)) - work[4][at] * curl
            moist = sum(q_buf[m, k, at].astype(jnp.float32) for m in range(members)) - slopes_ref[1:2, :] * heat
            for f, x in enumerate((curl, spread, heat, moist)):
                late_ref[c, k, :, f * levels : (f + 1) * levels] = (x * (1.0 / members)).astype(jnp.bfloat16)
    late_sends = scatter_means(late_ref, outs, EDGE, late_sems, len(outs))
    run(late_sends)
    finish(sends + late_sends)


def far_kernel(chunk, u_hbm, v_hbm, h_hbm, q_hbm, far_hbm, late_ref, psi_ref, bal_ref, slopes_ref, g_in_ref, g_ref, *scratch):
    u_ext, v_ext, h_buf, q_buf = scratch[:4]
    work = scratch[4:12]
    sems = scratch[12]
    core = core_index()
    copies = edge_copies(core, u_hbm, v_hbm, h_hbm, q_hbm, far_hbm, u_ext, v_ext, h_buf, q_buf, sems)
    run(copies)
    g_ref[...] = g_in_ref[...]
    finish(copies)
    row_from = (u_hbm.shape[1] - EDGE) * core
    compute_rows(EDGE, row_from, (u_ext, v_ext), (h_buf, q_buf), psi_ref, bal_ref, slopes_ref, work, g_ref, late_ref, True, chunk)


def halves_kernel(weight, g_in_ref, mine_ref, theirs_ref, g_ref):
    apart = (mine_ref[...].astype(jnp.float32) - theirs_ref[...].astype(jnp.float32)).astype(jnp.bfloat16)
    apart = apart.reshape(-1, apart.shape[2])
    half = g_ref.shape[0] // 2
    top = g_in_ref[0:half] + gram(apart[:, :half], apart) * weight
    g_ref[0:half] = top
    g_ref[half:, 0:half] = jnp.transpose(top[:, half:])
    g_ref[half:, half:] = g_in_ref[half:, half:] + gram(apart[:, half:], apart[:, half:]) * weight


def row_scratch(dims, n, ext):
    members, _, meridians, levels = dims
    return (
        [pltpu.VMEM((members, ext, meridians, levels), jnp.bfloat16)] * 2
        + [pltpu.VMEM((members, n, meridians, levels), jnp.bfloat16)] * 2
        + [pltpu.VMEM((members, meridians, 2 * levels), jnp.float32)] * 2
        + [pltpu.VMEM((meridians, levels), jnp.float32)] * 4
        + [pltpu.VMEM((members, meridians // 2, 4 * levels), jnp.bfloat16)] * 2
    )


def row_cost(dims, n):
    members, _, meridians, levels = dims
    return cost(4 * n * members * meridians * 16 * levels * levels, 8 << 20)


def between_kernel(members, g_in_ref, *rest):
    parts, (g_ref, mine_ref, theirs_ref) = rest[:-3], rest[-3:]
    side = lax.axis_index("member") % SIDE
    groups = len(parts) // 2
    g_ref[...] = g_in_ref[...]
    first = 0
    for part in (parts[:groups], parts[groups:]):
        _, n, chunk, width = part[0].shape
        overall = sum(p[...].astype(jnp.float32) for p in part) * (1.0 / groups)
        apart = [(p[...].astype(jnp.float32) - overall).astype(jnp.bfloat16).reshape(-1, width) for p in part]
        apart = jnp.concatenate(apart, axis=0)
        half = width // 2
        g_ref[0:half] += gram(apart[:, :half], apart) * float(members)
        g_ref[half:, half:] += gram(apart[:, half:], apart[:, half:]) * float(members)
        overall = overall.astype(jnp.bfloat16)
        low = side == 0
        mine_ref[first : first + n] = jnp.where(low, overall[0], overall[1])
        theirs_ref[first : first + n] = jnp.where(low, overall[1], overall[0])
        first += n


def on_device(u, v, h, q, psi, bal, slope_t, slope_q):
    dims = members, parallels, meridians, levels = u.shape
    width = 4 * levels
    count = lax.axis_size("space")
    peers = lax.axis_size("member")
    groups = peers // SIDE
    chunk = meridians // peers
    inner = parallels - 2 * EDGE
    slopes = jnp.stack([slope_t, slope_q])

    across = [(i, i + 1) for i in range(1, count - 1, 2)]
    across = across + [(b, a) for a, b in across]
    within = [(i, i + 1) for i in range(0, count, 2)]
    within = within + [(b, a) for a, b in within]

    def along_y(r):
        return [(y * SIDE + x, (y + r) % groups * SIDE + x) for y in range(groups) for x in range(SIDE)]

    along_x = [(y * SIDE + x, y * SIDE + 1 - x) for y in range(groups) for x in range(SIDE)]

    far_edge, near_edge, far_sums = edges_call(u, v)
    far_sums = lax.ppermute(far_sums, "space", across)
    far = lax.ppermute(far_edge, "space", across)
    near = lax.ppermute(near_edge, "space", within)

    g_shape = jax.ShapeDtypeStruct((width, width), jnp.float32)
    handed = lambda n: (jax.ShapeDtypeStruct((SIDE, n, chunk, width), jnp.bfloat16),) * groups

    dma = pltpu.SemaphoreType.DMA
    sum_shape = (3 * EDGE, meridians, levels)
    late_shape = jax.ShapeDtypeStruct((peers, EDGE, chunk, width), jnp.bfloat16)
    g, *means = pl.pallas_call(
        functools.partial(inner_kernel, chunk),
        name="inner_rows",
        out_shape=(g_shape,) + handed(inner),
        in_specs=[ANY] * 4 + [VMEM] * 3,
        out_specs=(VMEM,) + (ANY,) * groups,
        scratch_shapes=row_scratch(dims, inner, parallels)
        + [pltpu.VMEM((peers, inner, chunk, width), jnp.bfloat16), dma((4,)), dma((groups,))],
        compiler_params=params(22),
        cost_estimate=row_cost(dims, inner),
    )(u, v, in_hbm(h), in_hbm(q), psi, bal, slopes)
    means = [x if r == 0 else lax.ppermute(x, "member", along_y(r)) for r, x in enumerate(means)]

    g, late, *edge_means = pl.pallas_call(
        functools.partial(near_kernel, chunk),
        name="near_rows",
        out_shape=(g_shape, late_shape) + handed(2 * EDGE),
        in_specs=[ANY] * 5 + [VMEM] * 5,
        out_specs=(VMEM, VMEM) + (ANY,) * groups,
        scratch_shapes=row_scratch(dims, EDGE, 3 * EDGE)
        + [pltpu.VMEM((peers, EDGE, chunk, width), jnp.bfloat16)]
        + [pltpu.VMEM(sum_shape, jnp.float32)] * 2
        + [dma((6,)), dma((groups,)), dma((4,))]
        + row_scratch(dims, EDGE, 3 * EDGE)[:4],
        compiler_params=params(24),
        cost_estimate=row_cost(dims, EDGE),
    )(u, v, h, q, near, far_sums, psi, bal, slopes, g)
    edge_means = [x if r == 0 else lax.ppermute(x, "member", along_y(r)) for r, x in enumerate(edge_means)]

    half = jax.ShapeDtypeStruct((parallels, chunk, width), jnp.bfloat16)
    g, mine, theirs = pl.pallas_call(
        functools.partial(between_kernel, members),
        name="between",
        out_shape=(g_shape, half, half),
        in_specs=[VMEM] * (1 + 2 * groups),
        out_specs=(VMEM, VMEM, VMEM),
        compiler_params=params(16),
        cost_estimate=cost(1 << 30, 5 << 20),
    )(g, *means, *edge_means)
    theirs = lax.ppermute(theirs, "member", along_x)

    g = pl.pallas_call(
        functools.partial(far_kernel, chunk),
        name="far_rows",
        out_shape=g_shape,
        in_specs=[ANY] * 5 + [VMEM] * 5,
        out_specs=VMEM,
        scratch_shapes=row_scratch(dims, EDGE, 3 * EDGE) + [dma((6,))],
        compiler_params=params(16),
        cost_estimate=row_cost(dims, EDGE),
    )(u, v, h, q, far, late, psi, bal, slopes, g)

    g = pl.pallas_call(
        functools.partial(halves_kernel, members * groups / 2.0),
        name="halves",
        out_shape=g_shape,
        in_specs=[VMEM] * 3,
        out_specs=VMEM,
        compiler_params=params(8),
        cost_estimate=cost(1 << 28, 3 << 20),
    )(g, mine, theirs)

    parts = lax.all_to_all(g.reshape(peers, width // peers, width), "member", 0, 0, tiled=True)
    scale = 1.0 / ((members * peers - 1) * parallels * meridians)
    return (jnp.sum(parts, axis=0) * scale)[None]


def solution(mesh):
    placed = (P("member", "space", None, None),) * 4 + (P("space", None),) * 2 + (P(), P())
    return jax.shard_map(
        on_device, mesh=mesh, in_specs=placed, out_specs=P("space", "member", None), check_vma=False
    )
```

```python
import functools

import jax
import jax.numpy as jnp
from jax import lax
from jax.experimental import pallas as pl
from jax.experimental.pallas import tpu as pltpu
from jax.sharding import PartitionSpec as P

ANY = pl.BlockSpec(memory_space=pl.ANY)
VMEM = pl.BlockSpec(memory_space=pltpu.VMEM)
SIDE = 2
EDGE = 2


def params(mebibytes):
    return pltpu.CompilerParams(vmem_limit_bytes=mebibytes << 20)


def in_hbm(x):
    return pltpu.with_memory_space_constraint(x, pltpu.HBM)


def cost(flops, moved):
    return pl.CostEstimate(flops=flops, bytes_accessed=moved, transcendentals=0)


def gram(a, b):
    return lax.dot_general(a, b, (((0,), (0,)), ((), ())), preferred_element_type=jnp.float32)


def core_index():
    return lax.axis_index("space") % 2


def run(copies):
    for copy in copies:
        copy.start()


def finish(copies):
    for copy in copies:
        copy.wait()


def sums_kernel(u_hbm, v_hbm, sums_ref, rows, sems):
    at = pl.ds((u_hbm.shape[1] - EDGE) * core_index(), EDGE)
    copies = [pltpu.make_async_copy(x.at[:, at], rows.at[f], sems.at[f]) for f, x in enumerate((u_hbm, v_hbm))]
    run(copies)
    for f, copy in enumerate(copies):
        copy.wait()
        for r in range(EDGE):
            total = rows[f, 0, r].astype(jnp.float32)
            for m in range(1, rows.shape[1]):
                total = total + rows[f, m, r].astype(jnp.float32)
            sums_ref[f, r] = total.astype(jnp.bfloat16)


def edges_kernel(u_hbm, v_hbm, sums_hbm, far_ref, near_ref, sems):
    del sums_hbm
    core = core_index()
    far_at = pl.ds((u_hbm.shape[1] - EDGE) * core, EDGE)
    near_at = pl.ds((u_hbm.shape[1] - EDGE) * (1 - core), EDGE)
    copies = [pltpu.make_async_copy(x.at[:, far_at], far_ref.at[f], sems.at[f]) for f, x in enumerate((u_hbm, v_hbm))]
    copies += [pltpu.make_async_copy(x.at[:, near_at], near_ref.at[f], sems.at[2 + f]) for f, x in enumerate((u_hbm, v_hbm))]
    run(copies)
    finish(copies)


def edges_call(u, v):
    members, _, meridians, levels = u.shape
    edge = jax.ShapeDtypeStruct((2, members, EDGE, meridians, levels), u.dtype)
    sums = pl.pallas_call(
        sums_kernel,
        name="edge_sums",
        out_shape=jax.ShapeDtypeStruct((2, EDGE, meridians, levels), u.dtype),
        in_specs=[ANY, ANY],
        out_specs=VMEM,
        scratch_shapes=[pltpu.VMEM(edge.shape, u.dtype), pltpu.SemaphoreType.DMA((2,))],
        compiler_params=params(8),
        cost_estimate=cost(1 << 20, 3 << 20),
    )(in_hbm(u), in_hbm(v))
    far, near = pl.pallas_call(
        edges_kernel,
        name="edges",
        out_shape=(edge, edge),
        in_specs=[ANY, ANY, ANY],
        out_specs=(VMEM, VMEM),
        scratch_shapes=[pltpu.SemaphoreType.DMA((4,))],
        compiler_params=params(8),
        cost_estimate=cost(1 << 20, 6 << 20),
    )(in_hbm(u), in_hbm(v), sums)
    return far, near, sums


def spread_over(at, psi_ref, bal_ref, slope_t, levels):
    shape = (levels, psi_ref.shape[1])
    psi = jnp.transpose(jnp.broadcast_to(psi_ref[pl.ds(at, 1), :] * (1.0 / 12.0), shape))
    balance = jnp.transpose(jnp.broadcast_to(bal_ref[pl.ds(at, 1), :], shape))
    return psi, balance * slope_t


def lat_diff(rows):
    return (rows[2] - rows[1]) * 8.0 - (rows[3] - rows[0])


def add_gram(g_ref, a):
    half = a.shape[1] // 2
    g_ref[0:half] += gram(a[:, :half], a)
    g_ref[half:, half:] += gram(a[:, half:], a[:, half:])


def compute_rows(n, row_from, winds, scalars, psi_ref, bal_ref, slopes_ref, work, g_ref, m_ref, known, chunk, ready=lambda: None):
    u_ext, v_ext = winds
    h_buf, q_buf = scalars
    d_bufs, psi_bs, sb_bs, s_bufs = work[0:2], work[2:4], work[4:6], work[6:8]
    members, _, meridians, levels = u_ext.shape
    row = lax.broadcasted_iota(jnp.int32, (meridians, meridians), 0)
    col = lax.broadcasted_iota(jnp.int32, (meridians, meridians), 1)
    east = (row + 1) % meridians == col
    west = (row + meridians - 1) % meridians == col
    stencil = jnp.where(east, 6.0, jnp.where(west, -6.0, 0.0)).astype(jnp.bfloat16)
    slope_t = slopes_ref[0:1, :]
    slope_q = slopes_ref[1:2, :]
    half = meridians // 2
    cuts = [slice(f * levels, (f + 1) * levels) for f in range(4)]

    def prepare(k):
        b = k % 2
        psi_bs[b][...], sb_bs[b][...] = spread_over(row_from + k, psi_ref, bal_ref, slope_t, levels)
        for m in range(members):
            both = jnp.concatenate([v_ext[m, k + EDGE], u_ext[m, k + EDGE]], axis=1)
            d_bufs[b][m] = jnp.dot(stencil, both, preferred_element_type=jnp.float32)

    def derive(k, part):
        b = k % 2
        s_buf = s_bufs[part]
        for start in range(0, half, chunk):
            c = (part * half + start) // chunk
            at = slice(c * chunk, (c + 1) * chunk)
            to = slice(start, start + chunk)
            psi = psi_bs[b][at, :]
            sb = sb_bs[b][at, :]
            total = [None] * 4
            for m in range(members):
                du = lat_diff([u_ext[m, k + e, at, :].astype(jnp.float32) for e in (0, 1, 3, 4)])
                dv = lat_diff([v_ext[m, k + e, at, :].astype(jnp.float32) for e in (0, 1, 3, 4)])
                curl = psi * (d_bufs[b][m, at, 0:levels] - du)
                spread = psi * (d_bufs[b][m, at, levels : 2 * levels] + dv)
                heat = h_buf[m, k, at, :].astype(jnp.float32) - sb * curl
                moist = q_buf[m, k, at, :].astype(jnp.float32) - slope_q * heat
                for f, x in enumerate((curl, spread, heat, moist)):
                    x = x.astype(jnp.bfloat16)
                    if known:
                        mean = m_ref[c, k, :, cuts[f]].astype(jnp.float32)
                        s_buf[m, to, cuts[f]] = (x.astype(jnp.float32) - mean).astype(jnp.bfloat16)
                    else:
                        s_buf[m, to, cuts[f]] = x
                        x = x.astype(jnp.float32)
                        total[f] = x if m == 0 else total[f] + x
            if not known:
                for f, cut in enumerate(cuts):
                    mean = total[f] * (1.0 / members)
                    m_ref[c, k, :, cut] = mean.astype(jnp.bfloat16)
                    for m in range(members):
                        s_buf[m, to, cut] = (s_buf[m, to, cut].astype(jnp.float32) - mean).astype(jnp.bfloat16)

    def take(part):
        s_buf = s_bufs[part]
        add_gram(g_ref, s_buf[...].reshape(-1, s_buf.shape[2]))

    prepare(0)
    ready()
    for k in range(n):
        derive(k, 0)
        if k > 0:
            take(1)
        if k + 1 < n:
            prepare(k + 1)
        derive(k, 1)
        take(0)
    take(1)


def scatter_means(m_scr, outs, first, sem, groups):
    y = lax.axis_index("member") // SIDE
    n = m_scr.shape[1]
    return [
        pltpu.make_async_copy(
            m_scr.at[pl.ds(SIDE * lax.rem(y + r, groups), SIDE)], out.at[:, pl.ds(first, n)], sem.at[r]
        )
        for r, out in enumerate(outs)
    ]


def inner_kernel(chunk, u_hbm, v_hbm, h_hbm, q_hbm, psi_ref, bal_ref, slopes_ref, g_ref, *rest):
    outs, scratch = rest[:-15], rest[-15:]
    u_ext, v_ext, h_buf, q_buf = scratch[:4]
    work = scratch[4:12]
    m_scr, sems, out_sems = scratch[12:]
    n = m_scr.shape[1]
    inner = pl.ds(EDGE, n)
    pairs = ((u_hbm, u_ext), (v_hbm, v_ext), (h_hbm.at[:, inner], h_buf), (q_hbm.at[:, inner], q_buf))
    copies = [pltpu.make_async_copy(x, y, sems.at[i]) for i, (x, y) in enumerate(pairs)]
    run(copies)
    g_ref[...] = jnp.zeros_like(g_ref)
    finish(copies[:2])
    compute_rows(n, EDGE, (u_ext, v_ext), (h_buf, q_buf), psi_ref, bal_ref, slopes_ref, work, g_ref, m_scr, False, chunk, lambda: finish(copies[2:]))
    sends = scatter_means(m_scr, outs, 0, out_sems, len(outs))
    run(sends)
    finish(sends)


def edge_copies(side, u_hbm, v_hbm, h_hbm, q_hbm, halo, u_ext, v_ext, h_buf, q_buf, sems):
    parallels = u_hbm.shape[1]
    own = u_ext.shape[1] - EDGE
    own_from = pl.ds((parallels - own) * side, own)
    own_to = pl.ds(EDGE * (1 - side), own)
    halo_to = pl.ds(own * side, EDGE)
    row_from = pl.ds((parallels - EDGE) * side, EDGE)
    copies = [
        pltpu.make_async_copy(u_hbm.at[:, own_from], u_ext.at[:, own_to], sems.at[0]),
        pltpu.make_async_copy(v_hbm.at[:, own_from], v_ext.at[:, own_to], sems.at[1]),
        pltpu.make_async_copy(h_hbm.at[:, row_from], h_buf, sems.at[2]),
        pltpu.make_async_copy(q_hbm.at[:, row_from], q_buf, sems.at[3]),
    ]
    if halo is not None:
        copies.append(pltpu.make_async_copy(halo.at[0], u_ext.at[:, halo_to], sems.at[4]))
        copies.append(pltpu.make_async_copy(halo.at[1], v_ext.at[:, halo_to], sems.at[5]))
    return copies


def near_kernel(chunk, u_hbm, v_hbm, h_hbm, q_hbm, near_hbm, far_sums_ref, psi_ref, bal_ref, slopes_ref, g_in_ref, g_ref, late_ref, *rest):
    outs, scratch = rest[:-22], rest[-22:]
    u_ext, v_ext, h_buf, q_buf = scratch[:4]
    work = scratch[4:12]
    m_scr, u_sum, v_sum, sems, out_sems, late_sems = scratch[12:18]
    members, parallels, meridians, levels = u_hbm.shape
    side = 1 - core_index()
    copies = edge_copies(side, u_hbm, v_hbm, h_hbm, q_hbm, near_hbm, u_ext, v_ext, h_buf, q_buf, sems)
    run(copies)
    copies_far = edge_copies(1 - side, u_hbm, v_hbm, h_hbm, q_hbm, None, *scratch[18:22], late_sems)
    run(copies_far)
    g_ref[...] = g_in_ref[...]
    finish(copies)
    compute_rows(EDGE, (parallels - EDGE) * side, (u_ext, v_ext), (h_buf, q_buf), psi_ref, bal_ref, slopes_ref, work, g_ref, m_scr, False, chunk)
    sends = scatter_means(m_scr, outs, 0, out_sems, len(outs))
    run(sends)

    finish(copies_far)
    u_ext, v_ext, h_buf, q_buf = scratch[18:22]
    core = core_index()
    own = 2 * EDGE
    row_from = (parallels - EDGE) * core
    for f, (ext, total) in enumerate(((u_ext, u_sum), (v_ext, v_sum))):
        for r in range(EDGE):
            total[own * core + r] = far_sums_ref[f, r].astype(jnp.float32)
        for r in range(own):
            total[EDGE * (1 - core) + r] = sum(ext[m, EDGE * (1 - core) + r].astype(jnp.float32) for m in range(members))
    for k in range(EDGE):
        work[2][...], work[4][...] = spread_over(row_from + k, psi_ref, bal_ref, slopes_ref[0:1, :], levels)
        for c in range(meridians // chunk):
            at = slice(c * chunk, (c + 1) * chunk)
            du = lat_diff([u_sum[k + e, at] for e in (0, 1, 3, 4)])
            dv = lat_diff([v_sum[k + e, at] for e in (0, 1, 3, 4)])
            work[0][0, at, 0:levels] = du
            work[0][0, at, levels : 2 * levels] = dv
        east = [(pltpu.roll(x[k + EDGE], meridians - 1, 0) - pltpu.roll(x[k + EDGE], 1, 0)) * 6.0 for x in (v_sum, u_sum)]
        work[1][0, :, 0:levels] = east[0]
        work[1][0, :, levels : 2 * levels] = east[1]
        for c in range(meridians // chunk):
            at = slice(c * chunk, (c + 1) * chunk)
            psi = work[2][at]
            curl = psi * (work[1][0, at, 0:levels] - work[0][0, at, 0:levels])
            spread = psi * (work[1][0, at, levels : 2 * levels] + work[0][0, at, levels : 2 * levels])
            heat = sum(h_buf[m, k, at].astype(jnp.float32) for m in range(members)) - work[4][at] * curl
            moist = sum(q_buf[m, k, at].astype(jnp.float32) for m in range(members)) - slopes_ref[1:2, :] * heat
            for f, x in enumerate((curl, spread, heat, moist)):
                late_ref[c, k, :, f * levels : (f + 1) * levels] = (x * (1.0 / members)).astype(jnp.bfloat16)
    late_sends = scatter_means(late_ref, outs, EDGE, late_sems, len(outs))
    run(late_sends)
    finish(sends + late_sends)


def far_kernel(chunk, u_hbm, v_hbm, h_hbm, q_hbm, far_hbm, late_ref, psi_ref, bal_ref, slopes_ref, g_in_ref, g_ref, *scratch):
    u_ext, v_ext, h_buf, q_buf = scratch[:4]
    work = scratch[4:12]
    sems = scratch[12]
    core = core_index()
    copies = edge_copies(core, u_hbm, v_hbm, h_hbm, q_hbm, far_hbm, u_ext, v_ext, h_buf, q_buf, sems)
    run(copies)
    g_ref[...] = g_in_ref[...]
    finish(copies)
    row_from = (u_hbm.shape[1] - EDGE) * core
    compute_rows(EDGE, row_from, (u_ext, v_ext), (h_buf, q_buf), psi_ref, bal_ref, slopes_ref, work, g_ref, late_ref, True, chunk)


def halves_kernel(weight, g_in_ref, mine_ref, theirs_ref, g_ref):
    apart = (mine_ref[...].astype(jnp.float32) - theirs_ref[...].astype(jnp.float32)).astype(jnp.bfloat16)
    apart = apart.reshape(-1, apart.shape[2])
    half = g_ref.shape[0] // 2
    top = g_in_ref[0:half] + gram(apart[:, :half], apart) * weight
    g_ref[0:half] = top
    g_ref[half:, 0:half] = jnp.transpose(top[:, half:])
    g_ref[half:, half:] = g_in_ref[half:, half:] + gram(apart[:, half:], apart[:, half:]) * weight


def row_scratch(dims, n, ext):
    members, _, meridians, levels = dims
    return (
        [pltpu.VMEM((members, ext, meridians, levels), jnp.bfloat16)] * 2
        + [pltpu.VMEM((members, n, meridians, levels), jnp.bfloat16)] * 2
        + [pltpu.VMEM((members, meridians, 2 * levels), jnp.float32)] * 2
        + [pltpu.VMEM((meridians, levels), jnp.float32)] * 4
        + [pltpu.VMEM((members, meridians // 2, 4 * levels), jnp.bfloat16)] * 2
    )


def row_cost(dims, n):
    members, _, meridians, levels = dims
    return cost(16 * n * members * meridians * 16 * levels * levels, 32 << 20)


def between_kernel(members, g_in_ref, *rest):
    parts, (g_ref, mine_ref, theirs_ref) = rest[:-3], rest[-3:]
    side = lax.axis_index("member") % SIDE
    groups = len(parts) // 2
    g_ref[...] = g_in_ref[...]
    first = 0
    for part in (parts[:groups], parts[groups:]):
        _, n, chunk, width = part[0].shape
        overall = sum(p[...].astype(jnp.float32) for p in part) * (1.0 / groups)
        apart = [(p[...].astype(jnp.float32) - overall).astype(jnp.bfloat16).reshape(-1, width) for p in part]
        apart = jnp.concatenate(apart, axis=0)
        half = width // 2
        g_ref[0:half] += gram(apart[:, :half], apart) * float(members)
        g_ref[half:, half:] += gram(apart[:, half:], apart[:, half:]) * float(members)
        overall = overall.astype(jnp.bfloat16)
        low = side == 0
        mine_ref[first : first + n] = jnp.where(low, overall[0], overall[1])
        theirs_ref[first : first + n] = jnp.where(low, overall[1], overall[0])
        first += n


def on_device(u, v, h, q, psi, bal, slope_t, slope_q):
    dims = members, parallels, meridians, levels = u.shape
    width = 4 * levels
    count = lax.axis_size("space")
    peers = lax.axis_size("member")
    groups = peers // SIDE
    chunk = meridians // peers
    inner = parallels - 2 * EDGE
    slopes = jnp.stack([slope_t, slope_q])

    across = [(i, i + 1) for i in range(1, count - 1, 2)]
    across = across + [(b, a) for a, b in across]
    within = [(i, i + 1) for i in range(0, count, 2)]
    within = within + [(b, a) for a, b in within]

    def along_y(r):
        return [(y * SIDE + x, (y + r) % groups * SIDE + x) for y in range(groups) for x in range(SIDE)]

    along_x = [(y * SIDE + x, y * SIDE + 1 - x) for y in range(groups) for x in range(SIDE)]

    far_edge, near_edge, far_sums = edges_call(u, v)
    far_sums = lax.ppermute(far_sums, "space", across)
    far = lax.ppermute(far_edge, "space", across)
    near = lax.ppermute(near_edge, "space", within)

    g_shape = jax.ShapeDtypeStruct((width, width), jnp.float32)
    handed = lambda n: (jax.ShapeDtypeStruct((SIDE, n, chunk, width), jnp.bfloat16),) * groups

    dma = pltpu.SemaphoreType.DMA
    sum_shape = (3 * EDGE, meridians, levels)
    late_shape = jax.ShapeDtypeStruct((peers, EDGE, chunk, width), jnp.bfloat16)
    g, *means = pl.pallas_call(
        functools.partial(inner_kernel, chunk),
        name="inner_rows",
        out_shape=(g_shape,) + handed(inner),
        in_specs=[ANY] * 4 + [VMEM] * 3,
        out_specs=(VMEM,) + (ANY,) * groups,
        scratch_shapes=row_scratch(dims, inner, parallels)
        + [pltpu.VMEM((peers, inner, chunk, width), jnp.bfloat16), dma((4,)), dma((groups,))],
        compiler_params=params(22),
        cost_estimate=row_cost(dims, inner),
    )(u, v, in_hbm(h), in_hbm(q), psi, bal, slopes)
    means = [x if r == 0 else lax.ppermute(x, "member", along_y(r)) for r, x in enumerate(means)]

    g, late, *edge_means = pl.pallas_call(
        functools.partial(near_kernel, chunk),
        name="near_rows",
        out_shape=(g_shape, late_shape) + handed(2 * EDGE),
        in_specs=[ANY] * 5 + [VMEM] * 5,
        out_specs=(VMEM, VMEM) + (ANY,) * groups,
        scratch_shapes=row_scratch(dims, EDGE, 3 * EDGE)
        + [pltpu.VMEM((peers, EDGE, chunk, width), jnp.bfloat16)]
        + [pltpu.VMEM(sum_shape, jnp.float32)] * 2
        + [dma((6,)), dma((groups,)), dma((4,))]
        + row_scratch(dims, EDGE, 3 * EDGE)[:4],
        compiler_params=params(24),
        cost_estimate=row_cost(dims, EDGE),
    )(u, v, h, q, near, far_sums, psi, bal, slopes, g)
    edge_means = [x if r == 0 else lax.ppermute(x, "member", along_y(r)) for r, x in enumerate(edge_means)]

    half = jax.ShapeDtypeStruct((parallels, chunk, width), jnp.bfloat16)
    g, mine, theirs = pl.pallas_call(
        functools.partial(between_kernel, members),
        name="between",
        out_shape=(g_shape, half, half),
        in_specs=[VMEM] * (1 + 2 * groups),
        out_specs=(VMEM, VMEM, VMEM),
        compiler_params=params(16),
        cost_estimate=cost(1 << 30, 5 << 20),
    )(g, *means, *edge_means)
    theirs = lax.ppermute(theirs, "member", along_x)

    g = pl.pallas_call(
        functools.partial(far_kernel, chunk),
        name="far_rows",
        out_shape=g_shape,
        in_specs=[ANY] * 5 + [VMEM] * 5,
        out_specs=VMEM,
        scratch_shapes=row_scratch(dims, EDGE, 3 * EDGE) + [dma((6,))],
        compiler_params=params(16),
        cost_estimate=row_cost(dims, EDGE),
    )(u, v, h, q, far, late, psi, bal, slopes, g)

    g = pl.pallas_call(
        functools.partial(halves_kernel, members * groups / 2.0),
        name="halves",
        out_shape=g_shape,
        in_specs=[VMEM] * 3,
        out_specs=VMEM,
        compiler_params=params(8),
        cost_estimate=cost(1 << 28, 3 << 20),
    )(g, mine, theirs)

    parts = lax.all_to_all(g.reshape(peers, width // peers, width), "member", 0, 0, tiled=True)
    scale = 1.0 / ((members * peers - 1) * parallels * meridians)
    return (jnp.sum(parts, axis=0) * scale)[None]


def solution(mesh):
    placed = (P("member", "space", None, None),) * 4 + (P("space", None),) * 2 + (P(), P())
    return jax.shard_map(
        on_device, mesh=mesh, in_specs=placed, out_specs=P("space", "member", None), check_vma=False
    )
```

```python
import functools

import jax
import jax.numpy as jnp
from jax import lax
from jax.experimental import pallas as pl
from jax.experimental.pallas import tpu as pltpu
from jax.sharding import PartitionSpec as P

ANY = pl.BlockSpec(memory_space=pl.ANY)
VMEM = pl.BlockSpec(memory_space=pltpu.VMEM)
SIDE = 2
EDGE = 2


def params(mebibytes):
    return pltpu.CompilerParams(vmem_limit_bytes=mebibytes << 20)


def in_hbm(x):
    return pltpu.with_memory_space_constraint(x, pltpu.HBM)


def cost(flops, moved):
    return pl.CostEstimate(flops=flops, bytes_accessed=moved, transcendentals=0)


def gram(a, b):
    return lax.dot_general(a, b, (((0,), (0,)), ((), ())), preferred_element_type=jnp.float32)


def core_index():
    return lax.axis_index("space") % 2


def run(copies):
    for copy in copies:
        copy.start()


def finish(copies):
    for copy in copies:
        copy.wait()


def far_edge_kernel(u_hbm, v_hbm, far_ref, sums_ref, sems):
    at = pl.ds((u_hbm.shape[1] - EDGE) * core_index(), EDGE)
    copies = [pltpu.make_async_copy(x.at[:, at], far_ref.at[f], sems.at[f]) for f, x in enumerate((u_hbm, v_hbm))]
    run(copies)
    for f, copy in enumerate(copies):
        copy.wait()
        for r in range(EDGE):
            total = far_ref[f, 0, r].astype(jnp.float32)
            for m in range(1, far_ref.shape[1]):
                total = total + far_ref[f, m, r].astype(jnp.float32)
            sums_ref[f, r] = total.astype(jnp.bfloat16)


def near_edge_kernel(u_hbm, v_hbm, sums_hbm, near_ref, sems):
    del sums_hbm
    at = pl.ds((u_hbm.shape[1] - EDGE) * (1 - core_index()), EDGE)
    copies = [pltpu.make_async_copy(x.at[:, at], near_ref.at[f], sems.at[f]) for f, x in enumerate((u_hbm, v_hbm))]
    run(copies)
    finish(copies)


def edges_call(u, v):
    members, _, meridians, levels = u.shape
    edge = jax.ShapeDtypeStruct((2, members, EDGE, meridians, levels), u.dtype)
    far, sums = pl.pallas_call(
        far_edge_kernel,
        name="far_edge",
        out_shape=(edge, jax.ShapeDtypeStruct((2, EDGE, meridians, levels), u.dtype)),
        in_specs=[ANY, ANY],
        out_specs=(VMEM, VMEM),
        scratch_shapes=[pltpu.SemaphoreType.DMA((2,))],
        compiler_params=params(8),
        cost_estimate=cost(1 << 20, 3 << 20),
    )(in_hbm(u), in_hbm(v))
    near = pl.pallas_call(
        near_edge_kernel,
        name="near_edge",
        out_shape=edge,
        in_specs=[ANY, ANY, ANY],
        out_specs=VMEM,
        scratch_shapes=[pltpu.SemaphoreType.DMA((2,))],
        compiler_params=params(8),
        cost_estimate=cost(1 << 20, 3 << 20),
    )(in_hbm(u), in_hbm(v), sums)
    return far, near, sums


def spread_over(at, psi_ref, bal_ref, slope_t, levels):
    shape = (levels, psi_ref.shape[1])
    psi = jnp.transpose(jnp.broadcast_to(psi_ref[pl.ds(at, 1), :] * (1.0 / 12.0), shape))
    balance = jnp.transpose(jnp.broadcast_to(bal_ref[pl.ds(at, 1), :], shape))
    return psi, balance * slope_t


def lat_diff(rows):
    return (rows[2] - rows[1]) * 8.0 - (rows[3] - rows[0])


def add_gram(g_ref, a):
    half = a.shape[1] // 2
    g_ref[0:half] += gram(a[:, :half], a)
    g_ref[half:, half:] += gram(a[:, half:], a[:, half:])


def compute_rows(n, row_from, winds, scalars, psi_ref, bal_ref, slopes_ref, work, g_ref, m_ref, known, chunk, ready=lambda: None):
    u_ext, v_ext = winds
    h_buf, q_buf = scalars
    d_bufs, psi_bs, sb_bs, s_bufs = work[0:2], work[2:4], work[4:6], work[6:8]
    members, _, meridians, levels = u_ext.shape
    row = lax.broadcasted_iota(jnp.int32, (meridians, meridians), 0)
    col = lax.broadcasted_iota(jnp.int32, (meridians, meridians), 1)
    east = (row + 1) % meridians == col
    west = (row + meridians - 1) % meridians == col
    stencil = jnp.where(east, 6.0, jnp.where(west, -6.0, 0.0)).astype(jnp.bfloat16)
    slope_t = slopes_ref[0:1, :]
    slope_q = slopes_ref[1:2, :]
    half = meridians // 2
    cuts = [slice(f * levels, (f + 1) * levels) for f in range(4)]

    def prepare(k):
        b = k % 2
        psi_bs[b][...], sb_bs[b][...] = spread_over(row_from + k, psi_ref, bal_ref, slope_t, levels)
        for m in range(members):
            both = jnp.concatenate([v_ext[m, k + EDGE], u_ext[m, k + EDGE]], axis=1)
            d_bufs[b][m] = jnp.dot(stencil, both, preferred_element_type=jnp.float32)

    def derive(k, part):
        b = k % 2
        s_buf = s_bufs[part]
        for start in range(0, half, chunk):
            c = (part * half + start) // chunk
            at = slice(c * chunk, (c + 1) * chunk)
            to = slice(start, start + chunk)
            psi = psi_bs[b][at, :]
            sb = sb_bs[b][at, :]
            total = [None] * 4
            for m in range(members):
                du = lat_diff([u_ext[m, k + e, at, :].astype(jnp.float32) for e in (0, 1, 3, 4)])
                dv = lat_diff([v_ext[m, k + e, at, :].astype(jnp.float32) for e in (0, 1, 3, 4)])
                curl = psi * (d_bufs[b][m, at, 0:levels] - du)
                spread = psi * (d_bufs[b][m, at, levels : 2 * levels] + dv)
                heat = h_buf[m, k, at, :].astype(jnp.float32) - sb * curl
                moist = q_buf[m, k, at, :].astype(jnp.float32) - slope_q * heat
                for f, x in enumerate((curl, spread, heat, moist)):
                    x = x.astype(jnp.bfloat16)
                    if known:
                        mean = m_ref[c, k, :, cuts[f]].astype(jnp.float32)
                        s_buf[m, to, cuts[f]] = (x.astype(jnp.float32) - mean).astype(jnp.bfloat16)
                    else:
                        s_buf[m, to, cuts[f]] = x
                        x = x.astype(jnp.float32)
                        total[f] = x if m == 0 else total[f] + x
            if not known:
                for f, cut in enumerate(cuts):
                    mean = total[f] * (1.0 / members)
                    m_ref[c, k, :, cut] = mean.astype(jnp.bfloat16)
                    for m in range(members):
                        s_buf[m, to, cut] = (s_buf[m, to, cut].astype(jnp.float32) - mean).astype(jnp.bfloat16)

    def take(part):
        s_buf = s_bufs[part]
        add_gram(g_ref, s_buf[...].reshape(-1, s_buf.shape[2]))

    prepare(0)
    ready()
    for k in range(n):
        derive(k, 0)
        if k > 0:
            take(1)
        if k + 1 < n:
            prepare(k + 1)
        derive(k, 1)
        take(0)
    take(1)


def scatter_means(m_scr, outs, first, sem, groups):
    y = lax.axis_index("member") // SIDE
    n = m_scr.shape[1]
    return [
        pltpu.make_async_copy(
            m_scr.at[pl.ds(SIDE * lax.rem(y + r, groups), SIDE)], out.at[:, pl.ds(first, n)], sem.at[r]
        )
        for r, out in enumerate(outs)
    ]


def inner_kernel(chunk, u_hbm, v_hbm, h_hbm, q_hbm, psi_ref, bal_ref, slopes_ref, g_ref, *rest):
    outs, scratch = rest[:-15], rest[-15:]
    u_ext, v_ext, h_buf, q_buf = scratch[:4]
    work = scratch[4:12]
    m_scr, sems, out_sems = scratch[12:]
    n = m_scr.shape[1]
    inner = pl.ds(EDGE, n)
    pairs = ((u_hbm, u_ext), (v_hbm, v_ext), (h_hbm.at[:, inner], h_buf), (q_hbm.at[:, inner], q_buf))
    copies = [pltpu.make_async_copy(x, y, sems.at[i]) for i, (x, y) in enumerate(pairs)]
    run(copies)
    g_ref[...] = jnp.zeros_like(g_ref)
    finish(copies[:2])
    compute_rows(n, EDGE, (u_ext, v_ext), (h_buf, q_buf), psi_ref, bal_ref, slopes_ref, work, g_ref, m_scr, False, chunk, lambda: finish(copies[2:]))
    sends = scatter_means(m_scr, outs, 0, out_sems, len(outs))
    run(sends)
    finish(sends)


def edge_copies(side, u_hbm, v_hbm, h_hbm, q_hbm, halo, u_ext, v_ext, h_buf, q_buf, sems):
    parallels = u_hbm.shape[1]
    own = u_ext.shape[1] - EDGE
    own_from = pl.ds((parallels - own) * side, own)
    own_to = pl.ds(EDGE * (1 - side), own)
    halo_to = pl.ds(own * side, EDGE)
    row_from = pl.ds((parallels - EDGE) * side, EDGE)
    copies = [
        pltpu.make_async_copy(u_hbm.at[:, own_from], u_ext.at[:, own_to], sems.at[0]),
        pltpu.make_async_copy(v_hbm.at[:, own_from], v_ext.at[:, own_to], sems.at[1]),
        pltpu.make_async_copy(h_hbm.at[:, row_from], h_buf, sems.at[2]),
        pltpu.make_async_copy(q_hbm.at[:, row_from], q_buf, sems.at[3]),
    ]
    if halo is not None:
        copies.append(pltpu.make_async_copy(halo.at[0], u_ext.at[:, halo_to], sems.at[4]))
        copies.append(pltpu.make_async_copy(halo.at[1], v_ext.at[:, halo_to], sems.at[5]))
    return copies


def near_kernel(chunk, u_hbm, v_hbm, h_hbm, q_hbm, near_hbm, far_sums_ref, psi_ref, bal_ref, slopes_ref, g_in_ref, g_ref, late_ref, *rest):
    outs, scratch = rest[:-22], rest[-22:]
    u_ext, v_ext, h_buf, q_buf = scratch[:4]
    work = scratch[4:12]
    m_scr, u_sum, v_sum, sems, out_sems, late_sems = scratch[12:18]
    members, parallels, meridians, levels = u_hbm.shape
    side = 1 - core_index()
    copies = edge_copies(side, u_hbm, v_hbm, h_hbm, q_hbm, near_hbm, u_ext, v_ext, h_buf, q_buf, sems)
    run(copies)
    copies_far = edge_copies(1 - side, u_hbm, v_hbm, h_hbm, q_hbm, None, *scratch[18:22], late_sems)
    run(copies_far)
    g_ref[...] = g_in_ref[...]
    finish(copies)
    compute_rows(EDGE, (parallels - EDGE) * side, (u_ext, v_ext), (h_buf, q_buf), psi_ref, bal_ref, slopes_ref, work, g_ref, m_scr, False, chunk)
    sends = scatter_means(m_scr, outs, 0, out_sems, len(outs))
    run(sends)

    finish(copies_far)
    u_ext, v_ext, h_buf, q_buf = scratch[18:22]
    core = core_index()
    own = 2 * EDGE
    row_from = (parallels - EDGE) * core
    for f, (ext, total) in enumerate(((u_ext, u_sum), (v_ext, v_sum))):
        for r in range(EDGE):
            total[own * core + r] = far_sums_ref[f, r].astype(jnp.float32)
        for r in range(own):
            total[EDGE * (1 - core) + r] = sum(ext[m, EDGE * (1 - core) + r].astype(jnp.float32) for m in range(members))
    for k in range(EDGE):
        work[2][...], work[4][...] = spread_over(row_from + k, psi_ref, bal_ref, slopes_ref[0:1, :], levels)
        for c in range(meridians // chunk):
            at = slice(c * chunk, (c + 1) * chunk)
            du = lat_diff([u_sum[k + e, at] for e in (0, 1, 3, 4)])
            dv = lat_diff([v_sum[k + e, at] for e in (0, 1, 3, 4)])
            work[0][0, at, 0:levels] = du
            work[0][0, at, levels : 2 * levels] = dv
        east = [(pltpu.roll(x[k + EDGE], meridians - 1, 0) - pltpu.roll(x[k + EDGE], 1, 0)) * 6.0 for x in (v_sum, u_sum)]
        work[1][0, :, 0:levels] = east[0]
        work[1][0, :, levels : 2 * levels] = east[1]
        for c in range(meridians // chunk):
            at = slice(c * chunk, (c + 1) * chunk)
            psi = work[2][at]
            curl = psi * (work[1][0, at, 0:levels] - work[0][0, at, 0:levels])
            spread = psi * (work[1][0, at, levels : 2 * levels] + work[0][0, at, levels : 2 * levels])
            heat = sum(h_buf[m, k, at].astype(jnp.float32) for m in range(members)) - work[4][at] * curl
            moist = sum(q_buf[m, k, at].astype(jnp.float32) for m in range(members)) - slopes_ref[1:2, :] * heat
            for f, x in enumerate((curl, spread, heat, moist)):
                late_ref[c, k, :, f * levels : (f + 1) * levels] = (x * (1.0 / members)).astype(jnp.bfloat16)
    late_sends = scatter_means(late_ref, outs, EDGE, late_sems, len(outs))
    run(late_sends)
    finish(sends + late_sends)


def far_kernel(chunk, u_hbm, v_hbm, h_hbm, q_hbm, far_hbm, late_ref, psi_ref, bal_ref, slopes_ref, g_in_ref, g_ref, *scratch):
    u_ext, v_ext, h_buf, q_buf = scratch[:4]
    work = scratch[4:12]
    sems = scratch[12]
    core = core_index()
    copies = edge_copies(core, u_hbm, v_hbm, h_hbm, q_hbm, far_hbm, u_ext, v_ext, h_buf, q_buf, sems)
    run(copies)
    g_ref[...] = g_in_ref[...]
    finish(copies)
    row_from = (u_hbm.shape[1] - EDGE) * core
    compute_rows(EDGE, row_from, (u_ext, v_ext), (h_buf, q_buf), psi_ref, bal_ref, slopes_ref, work, g_ref, late_ref, True, chunk)


def halves_kernel(weight, g_in_ref, *rest):
    means, g_ref = rest[:-1], rest[-1]
    apart = [x[...].astype(jnp.float32) - y[...].astype(jnp.float32) for x, y in zip(means[::2], means[1::2])]
    apart = jnp.concatenate([x.astype(jnp.bfloat16).reshape(-1, x.shape[2]) for x in apart], axis=0)
    half = g_ref.shape[0] // 2
    top = g_in_ref[0:half] + gram(apart[:, :half], apart) * weight
    g_ref[0:half] = top
    g_ref[half:, 0:half] = jnp.transpose(top[:, half:])
    g_ref[half:, half:] = g_in_ref[half:, half:] + gram(apart[:, half:], apart[:, half:]) * weight


def row_scratch(dims, n, ext):
    members, _, meridians, levels = dims
    return (
        [pltpu.VMEM((members, ext, meridians, levels), jnp.bfloat16)] * 2
        + [pltpu.VMEM((members, n, meridians, levels), jnp.bfloat16)] * 2
        + [pltpu.VMEM((members, meridians, 2 * levels), jnp.float32)] * 2
        + [pltpu.VMEM((meridians, levels), jnp.float32)] * 4
        + [pltpu.VMEM((members, meridians // 2, 4 * levels), jnp.bfloat16)] * 2
    )


def row_cost(dims, n):
    members, _, meridians, levels = dims
    return cost(16 * n * members * meridians * 16 * levels * levels, 32 << 20)


def between_kernel(members, g_in_ref, *rest):
    parts, (g_ref, mine_ref, theirs_ref) = rest[:-3], rest[-3:]
    side = lax.axis_index("member") % SIDE
    groups = len(parts)
    _, n, chunk, width = parts[0].shape
    half = width // 2
    overall = sum(p[...].astype(jnp.float32) for p in parts) * (1.0 / groups)
    apart = [(p[...].astype(jnp.float32) - overall).astype(jnp.bfloat16).reshape(-1, width) for p in parts]
    apart = jnp.concatenate(apart, axis=0)
    g_ref[0:half] = g_in_ref[0:half] + gram(apart[:, :half], apart) * float(members)
    g_ref[half:, half:] = g_in_ref[half:, half:] + gram(apart[:, half:], apart[:, half:]) * float(members)
    overall = overall.astype(jnp.bfloat16)
    low = side == 0
    mine_ref[...] = jnp.where(low, overall[0], overall[1])
    theirs_ref[...] = jnp.where(low, overall[1], overall[0])


def on_device(u, v, h, q, psi, bal, slope_t, slope_q):
    dims = members, parallels, meridians, levels = u.shape
    width = 4 * levels
    count = lax.axis_size("space")
    peers = lax.axis_size("member")
    groups = peers // SIDE
    chunk = meridians // peers
    inner = parallels - 2 * EDGE
    slopes = jnp.stack([slope_t, slope_q])

    across = [(i, i + 1) for i in range(1, count - 1, 2)]
    across = across + [(b, a) for a, b in across]
    within = [(i, i + 1) for i in range(0, count, 2)]
    within = within + [(b, a) for a, b in within]

    def along_y(r):
        return [(y * SIDE + x, (y + r) % groups * SIDE + x) for y in range(groups) for x in range(SIDE)]

    along_x = [(y * SIDE + x, y * SIDE + 1 - x) for y in range(groups) for x in range(SIDE)]

    far_edge, near_edge, far_sums = edges_call(u, v)
    far_sums = lax.ppermute(far_sums, "space", across)
    far = lax.ppermute(far_edge, "space", across)
    near = lax.ppermute(near_edge, "space", within)

    g_shape = jax.ShapeDtypeStruct((width, width), jnp.float32)
    handed = lambda n: (jax.ShapeDtypeStruct((SIDE, n, chunk, width), jnp.bfloat16),) * groups

    dma = pltpu.SemaphoreType.DMA
    sum_shape = (3 * EDGE, meridians, levels)
    late_shape = jax.ShapeDtypeStruct((peers, EDGE, chunk, width), jnp.bfloat16)
    g, *means = pl.pallas_call(
        functools.partial(inner_kernel, chunk),
        name="inner_rows",
        out_shape=(g_shape,) + handed(inner),
        in_specs=[ANY] * 4 + [VMEM] * 3,
        out_specs=(VMEM,) + (ANY,) * groups,
        scratch_shapes=row_scratch(dims, inner, parallels)
        + [pltpu.VMEM((peers, inner, chunk, width), jnp.bfloat16), dma((4,)), dma((groups,))],
        compiler_params=params(22),
        cost_estimate=row_cost(dims, inner),
    )(u, v, in_hbm(h), in_hbm(q), psi, bal, slopes)
    means = [x if r == 0 else lax.ppermute(x, "member", along_y(r)) for r, x in enumerate(means)]

    g, late, *edge_means = pl.pallas_call(
        functools.partial(near_kernel, chunk),
        name="near_rows",
        out_shape=(g_shape, late_shape) + handed(2 * EDGE),
        in_specs=[ANY] * 5 + [VMEM] * 5,
        out_specs=(VMEM, VMEM) + (ANY,) * groups,
        scratch_shapes=row_scratch(dims, EDGE, 3 * EDGE)
        + [pltpu.VMEM((peers, EDGE, chunk, width), jnp.bfloat16)]
        + [pltpu.VMEM(sum_shape, jnp.float32)] * 2
        + [dma((6,)), dma((groups,)), dma((4,))]
        + row_scratch(dims, EDGE, 3 * EDGE)[:4],
        compiler_params=params(24),
        cost_estimate=row_cost(dims, EDGE),
    )(u, v, h, q, near, far_sums, psi, bal, slopes, g)
    edge_means = [x if r == 0 else lax.ppermute(x, "member", along_y(r)) for r, x in enumerate(edge_means)]

    halves = []
    for part in (means, edge_means):
        half = jax.ShapeDtypeStruct(part[0].shape[1:], jnp.bfloat16)
        g, mine, theirs = pl.pallas_call(
            functools.partial(between_kernel, members),
            name="between",
            out_shape=(g_shape, half, half),
            in_specs=[VMEM] * (1 + groups),
            out_specs=(VMEM, VMEM, VMEM),
            compiler_params=params(12),
            cost_estimate=cost(1 << 29, 3 << 20),
        )(g, *part)
        halves += [mine, lax.ppermute(theirs, "member", along_x)]

    g = pl.pallas_call(
        functools.partial(far_kernel, chunk),
        name="far_rows",
        out_shape=g_shape,
        in_specs=[ANY] * 5 + [VMEM] * 5,
        out_specs=VMEM,
        scratch_shapes=row_scratch(dims, EDGE, 3 * EDGE) + [dma((6,))],
        compiler_params=params(16),
        cost_estimate=row_cost(dims, EDGE),
    )(u, v, h, q, far, late, psi, bal, slopes, g)

    g = pl.pallas_call(
        functools.partial(halves_kernel, members * groups / 2.0),
        name="halves",
        out_shape=g_shape,
        in_specs=[VMEM] * (1 + len(halves)),
        out_specs=VMEM,
        compiler_params=params(8),
        cost_estimate=cost(1 << 28, 3 << 20),
    )(g, *halves)

    parts = lax.all_to_all(g.reshape(peers, width // peers, width), "member", 0, 0, tiled=True)
    scale = 1.0 / ((members * peers - 1) * parallels * meridians)
    return (jnp.sum(parts, axis=0) * scale)[None]


def solution(mesh):
    placed = (P("member", "space", None, None),) * 4 + (P("space", None),) * 2 + (P(), P())
    return jax.shard_map(
        on_device, mesh=mesh, in_specs=placed, out_specs=P("space", "member", None), check_vma=False
    )
```

```python
import functools

import jax
import jax.numpy as jnp
from jax import lax
from jax.experimental import pallas as pl
from jax.experimental.pallas import tpu as pltpu
from jax.sharding import PartitionSpec as P

ANY = pl.BlockSpec(memory_space=pl.ANY)
VMEM = pl.BlockSpec(memory_space=pltpu.VMEM)
SIDE = 2
EDGE = 2


def params(mebibytes):
    return pltpu.CompilerParams(vmem_limit_bytes=mebibytes << 20)


def in_hbm(x):
    return pltpu.with_memory_space_constraint(x, pltpu.HBM)


def cost(flops, moved):
    return pl.CostEstimate(flops=flops, bytes_accessed=moved, transcendentals=0)


def gram(a, b):
    return lax.dot_general(a, b, (((0,), (0,)), ((), ())), preferred_element_type=jnp.float32)


def core_index():
    return lax.axis_index("space") % 2


def run(copies):
    for copy in copies:
        copy.start()


def finish(copies):
    for copy in copies:
        copy.wait()


def far_edge_kernel(u_hbm, v_hbm, far_ref, sums_ref, sems):
    at = pl.ds((u_hbm.shape[1] - EDGE) * core_index(), EDGE)
    copies = [pltpu.make_async_copy(x.at[:, at], far_ref.at[f], sems.at[f]) for f, x in enumerate((u_hbm, v_hbm))]
    run(copies)
    for f, copy in enumerate(copies):
        copy.wait()
        for r in range(EDGE):
            total = far_ref[f, 0, r].astype(jnp.float32)
            for m in range(1, far_ref.shape[1]):
                total = total + far_ref[f, m, r].astype(jnp.float32)
            sums_ref[f, r] = total.astype(jnp.bfloat16)


def near_edge_kernel(u_hbm, v_hbm, sums_hbm, near_ref, sems):
    del sums_hbm
    at = pl.ds((u_hbm.shape[1] - EDGE) * (1 - core_index()), EDGE)
    copies = [pltpu.make_async_copy(x.at[:, at], near_ref.at[f], sems.at[f]) for f, x in enumerate((u_hbm, v_hbm))]
    run(copies)
    finish(copies)


def edges_call(u, v):
    members, _, meridians, levels = u.shape
    edge = jax.ShapeDtypeStruct((2, members, EDGE, meridians, levels), u.dtype)
    far, sums = pl.pallas_call(
        far_edge_kernel,
        name="far_edge",
        out_shape=(edge, jax.ShapeDtypeStruct((2, EDGE, meridians, levels), u.dtype)),
        in_specs=[ANY, ANY],
        out_specs=(VMEM, VMEM),
        scratch_shapes=[pltpu.SemaphoreType.DMA((2,))],
        compiler_params=params(8),
        cost_estimate=cost(1 << 20, 3 << 20),
    )(in_hbm(u), in_hbm(v))
    near = pl.pallas_call(
        near_edge_kernel,
        name="near_edge",
        out_shape=edge,
        in_specs=[ANY, ANY, ANY],
        out_specs=VMEM,
        scratch_shapes=[pltpu.SemaphoreType.DMA((2,))],
        compiler_params=params(8),
        cost_estimate=cost(1 << 20, 3 << 20),
    )(in_hbm(u), in_hbm(v), sums)
    return far, near, sums


def spread_over(at, psi_ref, bal_ref, slope_t, levels):
    shape = (levels, psi_ref.shape[1])
    psi = jnp.transpose(jnp.broadcast_to(psi_ref[pl.ds(at, 1), :] * (1.0 / 12.0), shape))
    balance = jnp.transpose(jnp.broadcast_to(bal_ref[pl.ds(at, 1), :], shape))
    return psi, balance * slope_t


def lat_diff(rows):
    return (rows[2] - rows[1]) * 8.0 - (rows[3] - rows[0])


def add_gram(g_ref, a):
    half = a.shape[1] // 2
    g_ref[0:half] += gram(a[:, :half], a)
    g_ref[half:, half:] += gram(a[:, half:], a[:, half:])


def compute_rows(n, row_from, winds, scalars, psi_ref, bal_ref, slopes_ref, work, g_ref, m_ref, known, chunk, ready=lambda: None):
    u_ext, v_ext = winds
    h_buf, q_buf = scalars
    d_bufs, psi_bs, sb_bs, s_bufs = work[0:2], work[2:4], work[4:6], work[6:8]
    members, _, meridians, levels = u_ext.shape
    row = lax.broadcasted_iota(jnp.int32, (meridians, meridians), 0)
    col = lax.broadcasted_iota(jnp.int32, (meridians, meridians), 1)
    east = (row + 1) % meridians == col
    west = (row + meridians - 1) % meridians == col
    stencil = jnp.where(east, 6.0, jnp.where(west, -6.0, 0.0)).astype(jnp.bfloat16)
    slope_t = slopes_ref[0:1, :]
    slope_q = slopes_ref[1:2, :]
    half = meridians // 2
    cuts = [slice(f * levels, (f + 1) * levels) for f in range(4)]

    def prepare(k):
        b = k % 2
        psi_bs[b][...], sb_bs[b][...] = spread_over(row_from + k, psi_ref, bal_ref, slope_t, levels)
        for m in range(members):
            both = jnp.concatenate([v_ext[m, k + EDGE], u_ext[m, k + EDGE]], axis=1)
            d_bufs[b][m] = jnp.dot(stencil, both, preferred_element_type=jnp.float32)

    def derive(k, part):
        b = k % 2
        s_buf = s_bufs[part]
        for start in range(0, half, chunk):
            c = (part * half + start) // chunk
            at = slice(c * chunk, (c + 1) * chunk)
            to = slice(start, start + chunk)
            psi = psi_bs[b][at, :]
            sb = sb_bs[b][at, :]
            total = [None] * 4
            for m in range(members):
                du = lat_diff([u_ext[m, k + e, at, :].astype(jnp.float32) for e in (0, 1, 3, 4)])
                dv = lat_diff([v_ext[m, k + e, at, :].astype(jnp.float32) for e in (0, 1, 3, 4)])
                curl = psi * (d_bufs[b][m, at, 0:levels] - du)
                spread = psi * (d_bufs[b][m, at, levels : 2 * levels] + dv)
                heat = h_buf[m, k, at, :].astype(jnp.float32) - sb * curl
                moist = q_buf[m, k, at, :].astype(jnp.float32) - slope_q * heat
                for f, x in enumerate((curl, spread, heat, moist)):
                    x = x.astype(jnp.bfloat16)
                    if known:
                        mean = m_ref[c, k, :, cuts[f]].astype(jnp.float32)
                        s_buf[m, to, cuts[f]] = (x.astype(jnp.float32) - mean).astype(jnp.bfloat16)
                    else:
                        s_buf[m, to, cuts[f]] = x
                        x = x.astype(jnp.float32)
                        total[f] = x if m == 0 else total[f] + x
            if not known:
                for f, cut in enumerate(cuts):
                    mean = total[f] * (1.0 / members)
                    m_ref[c, k, :, cut] = mean.astype(jnp.bfloat16)
                    for m in range(members):
                        s_buf[m, to, cut] = (s_buf[m, to, cut].astype(jnp.float32) - mean).astype(jnp.bfloat16)

    def take(part):
        s_buf = s_bufs[part]
        add_gram(g_ref, s_buf[...].reshape(-1, s_buf.shape[2]))

    prepare(0)
    ready()
    for k in range(n):
        derive(k, 0)
        if k > 0:
            take(1)
        if k + 1 < n:
            prepare(k + 1)
        derive(k, 1)
        take(0)
    take(1)


def scatter_means(m_scr, outs, first, sem, groups):
    y = lax.axis_index("member") // SIDE
    n = m_scr.shape[1]
    return [
        pltpu.make_async_copy(
            m_scr.at[pl.ds(SIDE * lax.rem(y + r, groups), SIDE)], out.at[:, pl.ds(first, n)], sem.at[r]
        )
        for r, out in enumerate(outs)
    ]


def inner_kernel(chunk, u_hbm, v_hbm, h_hbm, q_hbm, psi_ref, bal_ref, slopes_ref, g_ref, *rest):
    outs, scratch = rest[:-15], rest[-15:]
    u_ext, v_ext, h_buf, q_buf = scratch[:4]
    work = scratch[4:12]
    m_scr, sems, out_sems = scratch[12:]
    n = m_scr.shape[1]
    inner = pl.ds(EDGE, n)
    pairs = ((u_hbm, u_ext), (v_hbm, v_ext), (h_hbm.at[:, inner], h_buf), (q_hbm.at[:, inner], q_buf))
    copies = [pltpu.make_async_copy(x, y, sems.at[i]) for i, (x, y) in enumerate(pairs)]
    run(copies)
    g_ref[...] = jnp.zeros_like(g_ref)
    finish(copies[:2])
    compute_rows(n, EDGE, (u_ext, v_ext), (h_buf, q_buf), psi_ref, bal_ref, slopes_ref, work, g_ref, m_scr, False, chunk, lambda: finish(copies[2:]))
    sends = scatter_means(m_scr, outs, 0, out_sems, len(outs))
    run(sends)
    finish(sends)


def edge_copies(side, u_hbm, v_hbm, h_hbm, q_hbm, halo, u_ext, v_ext, h_buf, q_buf, sems):
    parallels = u_hbm.shape[1]
    own = u_ext.shape[1] - EDGE
    own_from = pl.ds((parallels - own) * side, own)
    own_to = pl.ds(EDGE * (1 - side), own)
    halo_to = pl.ds(own * side, EDGE)
    row_from = pl.ds((parallels - EDGE) * side, EDGE)
    copies = [
        pltpu.make_async_copy(u_hbm.at[:, own_from], u_ext.at[:, own_to], sems.at[0]),
        pltpu.make_async_copy(v_hbm.at[:, own_from], v_ext.at[:, own_to], sems.at[1]),
        pltpu.make_async_copy(h_hbm.at[:, row_from], h_buf, sems.at[2]),
        pltpu.make_async_copy(q_hbm.at[:, row_from], q_buf, sems.at[3]),
    ]
    if halo is not None:
        copies.append(pltpu.make_async_copy(halo.at[0], u_ext.at[:, halo_to], sems.at[4]))
        copies.append(pltpu.make_async_copy(halo.at[1], v_ext.at[:, halo_to], sems.at[5]))
    return copies


def near_kernel(chunk, u_hbm, v_hbm, h_hbm, q_hbm, near_hbm, psi_ref, bal_ref, slopes_ref, g_in_ref, g_ref, *rest):
    outs, scratch = rest[:-15], rest[-15:]
    u_ext, v_ext, h_buf, q_buf = scratch[:4]
    work = scratch[4:12]
    m_scr, sems, out_sems = scratch[12:]
    side = 1 - core_index()
    copies = edge_copies(side, u_hbm, v_hbm, h_hbm, q_hbm, near_hbm, u_ext, v_ext, h_buf, q_buf, sems)
    run(copies)
    g_ref[...] = g_in_ref[...]
    finish(copies)
    row_from = (u_hbm.shape[1] - EDGE) * side
    compute_rows(EDGE, row_from, (u_ext, v_ext), (h_buf, q_buf), psi_ref, bal_ref, slopes_ref, work, g_ref, m_scr, False, chunk)
    sends = scatter_means(m_scr, outs, 0, out_sems, len(outs))
    run(sends)
    finish(sends)


def far_means_kernel(chunk, u_hbm, v_hbm, h_hbm, q_hbm, after_hbm, far_sums_ref, psi_ref, bal_ref, slopes_ref, late_ref, *rest):
    del after_hbm
    outs, scratch = rest[:-14], rest[-14:]
    u_ext, v_ext, h_buf, q_buf = scratch[:4]
    work = scratch[4:10]
    u_sum, v_sum, sems, out_sems = scratch[10:]
    members, parallels, meridians, levels = u_hbm.shape
    copies = edge_copies(core_index(), u_hbm, v_hbm, h_hbm, q_hbm, None, u_ext, v_ext, h_buf, q_buf, sems)
    run(copies)
    finish(copies)
    core = core_index()
    own = 2 * EDGE
    row_from = (parallels - EDGE) * core
    for f, (ext, total) in enumerate(((u_ext, u_sum), (v_ext, v_sum))):
        for r in range(EDGE):
            total[own * core + r] = far_sums_ref[f, r].astype(jnp.float32)
        for r in range(own):
            total[EDGE * (1 - core) + r] = sum(ext[m, EDGE * (1 - core) + r].astype(jnp.float32) for m in range(members))
    for k in range(EDGE):
        work[2][...], work[4][...] = spread_over(row_from + k, psi_ref, bal_ref, slopes_ref[0:1, :], levels)
        for c in range(meridians // chunk):
            at = slice(c * chunk, (c + 1) * chunk)
            du = lat_diff([u_sum[k + e, at] for e in (0, 1, 3, 4)])
            dv = lat_diff([v_sum[k + e, at] for e in (0, 1, 3, 4)])
            work[0][0, at, 0:levels] = du
            work[0][0, at, levels : 2 * levels] = dv
        east = [(pltpu.roll(x[k + EDGE], meridians - 1, 0) - pltpu.roll(x[k + EDGE], 1, 0)) * 6.0 for x in (v_sum, u_sum)]
        work[1][0, :, 0:levels] = east[0]
        work[1][0, :, levels : 2 * levels] = east[1]
        for c in range(meridians // chunk):
            at = slice(c * chunk, (c + 1) * chunk)
            psi = work[2][at]
            curl = psi * (work[1][0, at, 0:levels] - work[0][0, at, 0:levels])
            spread = psi * (work[1][0, at, levels : 2 * levels] + work[0][0, at, levels : 2 * levels])
            heat = sum(h_buf[m, k, at].astype(jnp.float32) for m in range(members)) - work[4][at] * curl
            moist = sum(q_buf[m, k, at].astype(jnp.float32) for m in range(members)) - slopes_ref[1:2, :] * heat
            for f, x in enumerate((curl, spread, heat, moist)):
                late_ref[c, k, :, f * levels : (f + 1) * levels] = (x * (1.0 / members)).astype(jnp.bfloat16)
    sends = scatter_means(late_ref, outs, 0, out_sems, len(outs))
    run(sends)
    finish(sends)


def far_kernel(chunk, u_hbm, v_hbm, h_hbm, q_hbm, far_hbm, late_ref, psi_ref, bal_ref, slopes_ref, g_in_ref, g_ref, *scratch):
    u_ext, v_ext, h_buf, q_buf = scratch[:4]
    work = scratch[4:12]
    sems = scratch[12]
    core = core_index()
    copies = edge_copies(core, u_hbm, v_hbm, h_hbm, q_hbm, far_hbm, u_ext, v_ext, h_buf, q_buf, sems)
    run(copies)
    g_ref[...] = g_in_ref[...]
    finish(copies)
    row_from = (u_hbm.shape[1] - EDGE) * core
    compute_rows(EDGE, row_from, (u_ext, v_ext), (h_buf, q_buf), psi_ref, bal_ref, slopes_ref, work, g_ref, late_ref, True, chunk)


def halves_kernel(weight, g_in_ref, *rest):
    means, g_ref = rest[:-1], rest[-1]
    apart = [x[...].astype(jnp.float32) - y[...].astype(jnp.float32) for x, y in zip(means[::2], means[1::2])]
    apart = jnp.concatenate([x.astype(jnp.bfloat16).reshape(-1, x.shape[2]) for x in apart], axis=0)
    half = g_ref.shape[0] // 2
    top = g_in_ref[0:half] + gram(apart[:, :half], apart) * weight
    g_ref[0:half] = top
    g_ref[half:, 0:half] = jnp.transpose(top[:, half:])
    g_ref[half:, half:] = g_in_ref[half:, half:] + gram(apart[:, half:], apart[:, half:]) * weight


def row_scratch(dims, n, ext):
    members, _, meridians, levels = dims
    return (
        [pltpu.VMEM((members, ext, meridians, levels), jnp.bfloat16)] * 2
        + [pltpu.VMEM((members, n, meridians, levels), jnp.bfloat16)] * 2
        + [pltpu.VMEM((members, meridians, 2 * levels), jnp.float32)] * 2
        + [pltpu.VMEM((meridians, levels), jnp.float32)] * 4
        + [pltpu.VMEM((members, meridians // 2, 4 * levels), jnp.bfloat16)] * 2
    )


def row_cost(dims, n):
    members, _, meridians, levels = dims
    return cost(16 * n * members * meridians * 16 * levels * levels, 32 << 20)


def between_kernel(members, g_in_ref, *rest):
    parts, (g_ref, mine_ref, theirs_ref) = rest[:-3], rest[-3:]
    side = lax.axis_index("member") % SIDE
    groups = lax.axis_size("member") // SIDE
    width = parts[0].shape[3]
    half = width // 2
    low = side == 0
    apart = []
    first = 0
    for at in range(0, len(parts), groups):
        part = parts[at : at + groups]
        n = part[0].shape[1]
        overall = sum(p[...].astype(jnp.float32) for p in part) * (1.0 / groups)
        apart += [(p[...].astype(jnp.float32) - overall).astype(jnp.bfloat16).reshape(-1, width) for p in part]
        overall = overall.astype(jnp.bfloat16)
        mine_ref[first : first + n] = jnp.where(low, overall[0], overall[1])
        theirs_ref[first : first + n] = jnp.where(low, overall[1], overall[0])
        first += n
    apart = jnp.concatenate(apart, axis=0)
    g_ref[0:half] = g_in_ref[0:half] + gram(apart[:, :half], apart) * float(members)
    g_ref[half:, half:] = g_in_ref[half:, half:] + gram(apart[:, half:], apart[:, half:]) * float(members)


def on_device(u, v, h, q, psi, bal, slope_t, slope_q):
    dims = members, parallels, meridians, levels = u.shape
    width = 4 * levels
    count = lax.axis_size("space")
    peers = lax.axis_size("member")
    groups = peers // SIDE
    chunk = meridians // peers
    inner = parallels - 2 * EDGE
    slopes = jnp.stack([slope_t, slope_q])

    across = [(i, i + 1) for i in range(1, count - 1, 2)]
    across = across + [(b, a) for a, b in across]
    within = [(i, i + 1) for i in range(0, count, 2)]
    within = within + [(b, a) for a, b in within]

    def along_y(r):
        return [(y * SIDE + x, (y + r) % groups * SIDE + x) for y in range(groups) for x in range(SIDE)]

    along_x = [(y * SIDE + x, y * SIDE + 1 - x) for y in range(groups) for x in range(SIDE)]

    far_edge, near_edge, far_sums = edges_call(u, v)
    far_sums = lax.ppermute(far_sums, "space", across)
    far = lax.ppermute(far_edge, "space", across)
    near = lax.ppermute(near_edge, "space", within)

    g_shape = jax.ShapeDtypeStruct((width, width), jnp.float32)
    handed = lambda n: (jax.ShapeDtypeStruct((SIDE, n, chunk, width), jnp.bfloat16),) * groups

    dma = pltpu.SemaphoreType.DMA
    sum_shape = (3 * EDGE, meridians, levels)
    late_shape = jax.ShapeDtypeStruct((peers, EDGE, chunk, width), jnp.bfloat16)
    g, *means = pl.pallas_call(
        functools.partial(inner_kernel, chunk),
        name="inner_rows",
        out_shape=(g_shape,) + handed(inner),
        in_specs=[ANY] * 4 + [VMEM] * 3,
        out_specs=(VMEM,) + (ANY,) * groups,
        scratch_shapes=row_scratch(dims, inner, parallels)
        + [pltpu.VMEM((peers, inner, chunk, width), jnp.bfloat16), dma((4,)), dma((groups,))],
        compiler_params=params(22),
        cost_estimate=row_cost(dims, inner),
    )(u, v, in_hbm(h), in_hbm(q), psi, bal, slopes)
    means = [x if r == 0 else lax.ppermute(x, "member", along_y(r)) for r, x in enumerate(means)]

    g, *near_means = pl.pallas_call(
        functools.partial(near_kernel, chunk),
        name="near_rows",
        out_shape=(g_shape,) + handed(EDGE),
        in_specs=[ANY] * 5 + [VMEM] * 4,
        out_specs=(VMEM,) + (ANY,) * groups,
        scratch_shapes=row_scratch(dims, EDGE, 3 * EDGE)
        + [pltpu.VMEM((peers, EDGE, chunk, width), jnp.bfloat16), dma((6,)), dma((groups,))],
        compiler_params=params(16),
        cost_estimate=row_cost(dims, EDGE),
    )(u, v, h, q, near, psi, bal, slopes, g)
    after = near_means[0]
    near_means = [x if r == 0 else lax.ppermute(x, "member", along_y(r)) for r, x in enumerate(near_means)]

    late, *far_means = pl.pallas_call(
        functools.partial(far_means_kernel, chunk),
        name="far_means",
        out_shape=(late_shape,) + handed(EDGE),
        in_specs=[ANY] * 5 + [VMEM] * 4,
        out_specs=(VMEM,) + (ANY,) * groups,
        scratch_shapes=row_scratch(dims, EDGE, 3 * EDGE)[:10]
        + [pltpu.VMEM(sum_shape, jnp.float32)] * 2
        + [dma((4,)), dma((groups,))],
        compiler_params=params(14),
        cost_estimate=row_cost(dims, EDGE),
    )(u, v, h, q, after, far_sums, psi, bal, slopes)
    far_means = [x if r == 0 else lax.ppermute(x, "member", along_y(r)) for r, x in enumerate(far_means)]

    halves = []
    for part in (means + near_means, far_means):
        rows = sum(x.shape[1] for x in part[::groups])
        half = jax.ShapeDtypeStruct((rows, chunk, width), jnp.bfloat16)
        g, mine, theirs = pl.pallas_call(
            functools.partial(between_kernel, members),
            name="between",
            out_shape=(g_shape, half, half),
            in_specs=[VMEM] * (1 + len(part)),
            out_specs=(VMEM, VMEM, VMEM),
            compiler_params=params(12),
            cost_estimate=cost(1 << 29, 3 << 20),
        )(g, *part)
        halves += [mine, lax.ppermute(theirs, "member", along_x)]

    g = pl.pallas_call(
        functools.partial(far_kernel, chunk),
        name="far_rows",
        out_shape=g_shape,
        in_specs=[ANY] * 5 + [VMEM] * 5,
        out_specs=VMEM,
        scratch_shapes=row_scratch(dims, EDGE, 3 * EDGE) + [dma((6,))],
        compiler_params=params(16),
        cost_estimate=row_cost(dims, EDGE),
    )(u, v, h, q, far, late, psi, bal, slopes, g)

    g = pl.pallas_call(
        functools.partial(halves_kernel, members * groups / 2.0),
        name="halves",
        out_shape=g_shape,
        in_specs=[VMEM] * (1 + len(halves)),
        out_specs=VMEM,
        compiler_params=params(8),
        cost_estimate=cost(1 << 28, 3 << 20),
    )(g, *halves)

    parts = lax.all_to_all(g.reshape(peers, width // peers, width), "member", 0, 0, tiled=True)
    scale = 1.0 / ((members * peers - 1) * parallels * meridians)
    return (jnp.sum(parts, axis=0) * scale)[None]


def solution(mesh):
    placed = (P("member", "space", None, None),) * 4 + (P("space", None),) * 2 + (P(), P())
    return jax.shard_map(
        on_device, mesh=mesh, in_specs=placed, out_specs=P("space", "member", None), check_vma=False
    )
```

```python
import functools

import jax
import jax.numpy as jnp
from jax import lax
from jax.experimental import pallas as pl
from jax.experimental.pallas import tpu as pltpu
from jax.sharding import PartitionSpec as P

ANY = pl.BlockSpec(memory_space=pl.ANY)
VMEM = pl.BlockSpec(memory_space=pltpu.VMEM)
SIDE = 2
EDGE = 2


def params(mebibytes):
    return pltpu.CompilerParams(vmem_limit_bytes=mebibytes << 20)


def in_hbm(x):
    return pltpu.with_memory_space_constraint(x, pltpu.HBM)


def cost(flops, moved):
    return pl.CostEstimate(flops=flops, bytes_accessed=moved, transcendentals=0)


def gram(a, b):
    return lax.dot_general(a, b, (((0,), (0,)), ((), ())), preferred_element_type=jnp.float32)


def core_index():
    return lax.axis_index("space") % 2


def run(copies):
    for copy in copies:
        copy.start()


def finish(copies):
    for copy in copies:
        copy.wait()


def edges_kernel(u_hbm, v_hbm, far_ref, near_ref, sums_ref, sems):
    parallels = u_hbm.shape[1]
    core = core_index()
    winds = tuple(enumerate((u_hbm, v_hbm)))
    far_at = pl.ds((parallels - EDGE) * core, EDGE)
    near_at = pl.ds((parallels - EDGE) * (1 - core), EDGE)
    far = [pltpu.make_async_copy(x.at[:, far_at], far_ref.at[f], sems.at[f]) for f, x in winds]
    near = [pltpu.make_async_copy(x.at[:, near_at], near_ref.at[f], sems.at[2 + f]) for f, x in winds]
    run(far + near)
    for f, copy in enumerate(far):
        copy.wait()
        for r in range(EDGE):
            total = far_ref[f, 0, r].astype(jnp.float32)
            for m in range(1, far_ref.shape[1]):
                total = total + far_ref[f, m, r].astype(jnp.float32)
            sums_ref[f, r] = total.astype(jnp.bfloat16)
    finish(near)


def edges_call(u, v):
    members, _, meridians, levels = u.shape
    edge = jax.ShapeDtypeStruct((2, members, EDGE, meridians, levels), u.dtype)
    return pl.pallas_call(
        edges_kernel,
        name="edges",
        out_shape=(edge, edge, jax.ShapeDtypeStruct((2, EDGE, meridians, levels), u.dtype)),
        in_specs=[ANY, ANY],
        out_specs=(VMEM, VMEM, VMEM),
        scratch_shapes=[pltpu.SemaphoreType.DMA((4,))],
        compiler_params=params(8),
        cost_estimate=cost(1 << 20, 6 << 20),
    )(in_hbm(u), in_hbm(v))


def spread_over(at, psi_ref, bal_ref, slope_t, levels):
    shape = (levels, psi_ref.shape[1])
    psi = jnp.transpose(jnp.broadcast_to(psi_ref[pl.ds(at, 1), :] * (1.0 / 12.0), shape))
    balance = jnp.transpose(jnp.broadcast_to(bal_ref[pl.ds(at, 1), :], shape))
    return psi, balance * slope_t


def lat_diff(rows):
    return (rows[2] - rows[1]) * 8.0 - (rows[3] - rows[0])


def add_gram(g_ref, a):
    half = a.shape[1] // 2
    g_ref[0:half] += gram(a[:, :half], a)
    g_ref[half:, half:] += gram(a[:, half:], a[:, half:])


def compute_rows(n, row_from, winds, scalars, psi_ref, bal_ref, slopes_ref, work, g_ref, m_ref, known, chunk, ready=lambda: None):
    u_ext, v_ext = winds
    h_buf, q_buf = scalars
    d_bufs, psi_bs, sb_bs, s_bufs = work[0:2], work[2:4], work[4:6], work[6:8]
    members, _, meridians, levels = u_ext.shape
    row = lax.broadcasted_iota(jnp.int32, (meridians, meridians), 0)
    col = lax.broadcasted_iota(jnp.int32, (meridians, meridians), 1)
    east = (row + 1) % meridians == col
    west = (row + meridians - 1) % meridians == col
    stencil = jnp.where(east, 6.0, jnp.where(west, -6.0, 0.0)).astype(jnp.bfloat16)
    slope_t = slopes_ref[0:1, :]
    slope_q = slopes_ref[1:2, :]
    half = meridians // 2
    cuts = [slice(f * levels, (f + 1) * levels) for f in range(4)]

    def prepare(k):
        b = k % 2
        psi_bs[b][...], sb_bs[b][...] = spread_over(row_from + k, psi_ref, bal_ref, slope_t, levels)
        for m in range(members):
            both = jnp.concatenate([v_ext[m, k + EDGE], u_ext[m, k + EDGE]], axis=1)
            d_bufs[b][m] = jnp.dot(stencil, both, preferred_element_type=jnp.float32)

    def derive(k, part):
        b = k % 2
        s_buf = s_bufs[part]
        for start in range(0, half, chunk):
            c = (part * half + start) // chunk
            at = slice(c * chunk, (c + 1) * chunk)
            to = slice(start, start + chunk)
            psi = psi_bs[b][at, :]
            sb = sb_bs[b][at, :]
            total = [None] * 4
            for m in range(members):
                du = lat_diff([u_ext[m, k + e, at, :].astype(jnp.float32) for e in (0, 1, 3, 4)])
                dv = lat_diff([v_ext[m, k + e, at, :].astype(jnp.float32) for e in (0, 1, 3, 4)])
                curl = psi * (d_bufs[b][m, at, 0:levels] - du)
                spread = psi * (d_bufs[b][m, at, levels : 2 * levels] + dv)
                heat = h_buf[m, k, at, :].astype(jnp.float32) - sb * curl
                moist = q_buf[m, k, at, :].astype(jnp.float32) - slope_q * heat
                for f, x in enumerate((curl, spread, heat, moist)):
                    x = x.astype(jnp.bfloat16)
                    if known:
                        mean = m_ref[c, k, :, cuts[f]].astype(jnp.float32)
                        s_buf[m, to, cuts[f]] = (x.astype(jnp.float32) - mean).astype(jnp.bfloat16)
                    else:
                        s_buf[m, to, cuts[f]] = x
                        x = x.astype(jnp.float32)
                        total[f] = x if m == 0 else total[f] + x
            if not known:
                for f, cut in enumerate(cuts):
                    mean = total[f] * (1.0 / members)
                    m_ref[c, k, :, cut] = mean.astype(jnp.bfloat16)
                    for m in range(members):
                        s_buf[m, to, cut] = (s_buf[m, to, cut].astype(jnp.float32) - mean).astype(jnp.bfloat16)

    def take(part):
        s_buf = s_bufs[part]
        add_gram(g_ref, s_buf[...].reshape(-1, s_buf.shape[2]))

    prepare(0)
    ready()
    for k in range(n):
        derive(k, 0)
        if k > 0:
            take(1)
        if k + 1 < n:
            prepare(k + 1)
        derive(k, 1)
        take(0)
    take(1)


def scatter_means(m_scr, outs, first, sem, groups):
    y = lax.axis_index("member") // SIDE
    n = m_scr.shape[1]
    return [
        pltpu.make_async_copy(
            m_scr.at[pl.ds(SIDE * lax.rem(y + r, groups), SIDE)], out.at[:, pl.ds(first, n)], sem.at[r]
        )
        for r, out in enumerate(outs)
    ]


def early_kernel(chunk, u_hbm, v_hbm, h_hbm, q_hbm, near_hbm, psi_ref, bal_ref, slopes_ref, g_ref, *rest):
    outs, scratch = rest[:-15], rest[-15:]
    u_ext, v_ext, h_buf, q_buf = scratch[:4]
    work = scratch[4:12]
    m_scr, sems, out_sems = scratch[12:]
    parallels = u_hbm.shape[1]
    n = m_scr.shape[1]
    core = core_index()
    own_to = pl.ds(EDGE * core, parallels)
    near_to = pl.ds(parallels * (1 - core), EDGE)
    row_from = EDGE * (1 - core)
    rows = pl.ds(row_from, n)
    pairs = [(u_hbm, u_ext.at[:, own_to]), (v_hbm, v_ext.at[:, own_to])]
    pairs += [(near_hbm.at[0], u_ext.at[:, near_to]), (near_hbm.at[1], v_ext.at[:, near_to])]
    pairs += [(h_hbm.at[:, rows], h_buf), (q_hbm.at[:, rows], q_buf)]
    copies = [pltpu.make_async_copy(x, y, sems.at[i]) for i, (x, y) in enumerate(pairs)]
    run(copies)
    g_ref[...] = jnp.zeros_like(g_ref)
    finish(copies[:4])
    ready = lambda: finish(copies[4:])
    compute_rows(n, row_from, (u_ext, v_ext), (h_buf, q_buf), psi_ref, bal_ref, slopes_ref, work, g_ref, m_scr, False, chunk, ready)
    sends = scatter_means(m_scr, outs, 0, out_sems, len(outs))
    run(sends)
    finish(sends)


def edge_copies(side, u_hbm, v_hbm, h_hbm, q_hbm, halo, u_ext, v_ext, h_buf, q_buf, sems):
    parallels = u_hbm.shape[1]
    own = u_ext.shape[1] - EDGE
    own_from = pl.ds((parallels - own) * side, own)
    own_to = pl.ds(EDGE * (1 - side), own)
    halo_to = pl.ds(own * side, EDGE)
    row_from = pl.ds((parallels - EDGE) * side, EDGE)
    copies = [
        pltpu.make_async_copy(u_hbm.at[:, own_from], u_ext.at[:, own_to], sems.at[0]),
        pltpu.make_async_copy(v_hbm.at[:, own_from], v_ext.at[:, own_to], sems.at[1]),
        pltpu.make_async_copy(h_hbm.at[:, row_from], h_buf, sems.at[2]),
        pltpu.make_async_copy(q_hbm.at[:, row_from], q_buf, sems.at[3]),
    ]
    if halo is not None:
        copies.append(pltpu.make_async_copy(halo.at[0], u_ext.at[:, halo_to], sems.at[4]))
        copies.append(pltpu.make_async_copy(halo.at[1], v_ext.at[:, halo_to], sems.at[5]))
    return copies


def far_means_kernel(chunk, u_hbm, v_hbm, h_hbm, q_hbm, after_hbm, far_sums_ref, psi_ref, bal_ref, slopes_ref, late_ref, *rest):
    del after_hbm
    outs, scratch = rest[:-14], rest[-14:]
    u_ext, v_ext, h_buf, q_buf = scratch[:4]
    work = scratch[4:10]
    u_sum, v_sum, sems, out_sems = scratch[10:]
    members, parallels, meridians, levels = u_hbm.shape
    copies = edge_copies(core_index(), u_hbm, v_hbm, h_hbm, q_hbm, None, u_ext, v_ext, h_buf, q_buf, sems)
    run(copies)
    finish(copies)
    core = core_index()
    own = 2 * EDGE
    row_from = (parallels - EDGE) * core
    for f, (ext, total) in enumerate(((u_ext, u_sum), (v_ext, v_sum))):
        for r in range(EDGE):
            total[own * core + r] = far_sums_ref[f, r].astype(jnp.float32)
        for r in range(own):
            total[EDGE * (1 - core) + r] = sum(ext[m, EDGE * (1 - core) + r].astype(jnp.float32) for m in range(members))
    for k in range(EDGE):
        work[2][...], work[4][...] = spread_over(row_from + k, psi_ref, bal_ref, slopes_ref[0:1, :], levels)
        for c in range(meridians // chunk):
            at = slice(c * chunk, (c + 1) * chunk)
            du = lat_diff([u_sum[k + e, at] for e in (0, 1, 3, 4)])
            dv = lat_diff([v_sum[k + e, at] for e in (0, 1, 3, 4)])
            work[0][0, at, 0:levels] = du
            work[0][0, at, levels : 2 * levels] = dv
        east = [(pltpu.roll(x[k + EDGE], meridians - 1, 0) - pltpu.roll(x[k + EDGE], 1, 0)) * 6.0 for x in (v_sum, u_sum)]
        work[1][0, :, 0:levels] = east[0]
        work[1][0, :, levels : 2 * levels] = east[1]
        for c in range(meridians // chunk):
            at = slice(c * chunk, (c + 1) * chunk)
            psi = work[2][at]
            curl = psi * (work[1][0, at, 0:levels] - work[0][0, at, 0:levels])
            spread = psi * (work[1][0, at, levels : 2 * levels] + work[0][0, at, levels : 2 * levels])
            heat = sum(h_buf[m, k, at].astype(jnp.float32) for m in range(members)) - work[4][at] * curl
            moist = sum(q_buf[m, k, at].astype(jnp.float32) for m in range(members)) - slopes_ref[1:2, :] * heat
            for f, x in enumerate((curl, spread, heat, moist)):
                late_ref[c, k, :, f * levels : (f + 1) * levels] = (x * (1.0 / members)).astype(jnp.bfloat16)
    sends = scatter_means(late_ref, outs, 0, out_sems, len(outs))
    run(sends)
    finish(sends)


def far_kernel(chunk, u_hbm, v_hbm, h_hbm, q_hbm, far_hbm, late_ref, psi_ref, bal_ref, slopes_ref, g_in_ref, g_ref, *scratch):
    u_ext, v_ext, h_buf, q_buf = scratch[:4]
    work = scratch[4:12]
    sems = scratch[12]
    core = core_index()
    copies = edge_copies(core, u_hbm, v_hbm, h_hbm, q_hbm, far_hbm, u_ext, v_ext, h_buf, q_buf, sems)
    run(copies)
    g_ref[...] = g_in_ref[...]
    finish(copies)
    row_from = (u_hbm.shape[1] - EDGE) * core
    compute_rows(EDGE, row_from, (u_ext, v_ext), (h_buf, q_buf), psi_ref, bal_ref, slopes_ref, work, g_ref, late_ref, True, chunk)


def halves_kernel(weight, g_in_ref, *rest):
    means, g_ref = rest[:-1], rest[-1]
    apart = [x[...].astype(jnp.float32) - y[...].astype(jnp.float32) for x, y in zip(means[::2], means[1::2])]
    apart = jnp.concatenate([x.astype(jnp.bfloat16).reshape(-1, x.shape[2]) for x in apart], axis=0)
    half = g_ref.shape[0] // 2
    top = g_in_ref[0:half] + gram(apart[:, :half], apart) * weight
    g_ref[0:half] = top
    g_ref[half:, 0:half] = jnp.transpose(top[:, half:])
    g_ref[half:, half:] = g_in_ref[half:, half:] + gram(apart[:, half:], apart[:, half:]) * weight


def row_scratch(dims, n, ext):
    members, _, meridians, levels = dims
    return (
        [pltpu.VMEM((members, ext, meridians, levels), jnp.bfloat16)] * 2
        + [pltpu.VMEM((members, n, meridians, levels), jnp.bfloat16)] * 2
        + [pltpu.VMEM((members, meridians, 2 * levels), jnp.float32)] * 2
        + [pltpu.VMEM((meridians, levels), jnp.float32)] * 4
        + [pltpu.VMEM((members, meridians // 2, 4 * levels), jnp.bfloat16)] * 2
    )


def row_cost(dims, n):
    members, _, meridians, levels = dims
    return cost(16 * n * members * meridians * 16 * levels * levels, 32 << 20)


def between_kernel(members, g_in_ref, *rest):
    parts, (g_ref, mine_ref, theirs_ref) = rest[:-3], rest[-3:]
    side = lax.axis_index("member") % SIDE
    groups = lax.axis_size("member") // SIDE
    width = parts[0].shape[3]
    half = width // 2
    low = side == 0
    apart = []
    first = 0
    for at in range(0, len(parts), groups):
        part = parts[at : at + groups]
        n = part[0].shape[1]
        overall = sum(p[...].astype(jnp.float32) for p in part) * (1.0 / groups)
        apart += [(p[...].astype(jnp.float32) - overall).astype(jnp.bfloat16).reshape(-1, width) for p in part]
        overall = overall.astype(jnp.bfloat16)
        mine_ref[first : first + n] = jnp.where(low, overall[0], overall[1])
        theirs_ref[first : first + n] = jnp.where(low, overall[1], overall[0])
        first += n
    apart = jnp.concatenate(apart, axis=0)
    g_ref[0:half] = g_in_ref[0:half] + gram(apart[:, :half], apart) * float(members)
    g_ref[half:, half:] = g_in_ref[half:, half:] + gram(apart[:, half:], apart[:, half:]) * float(members)


def on_device(u, v, h, q, psi, bal, slope_t, slope_q):
    dims = members, parallels, meridians, levels = u.shape
    width = 4 * levels
    count = lax.axis_size("space")
    peers = lax.axis_size("member")
    groups = peers // SIDE
    chunk = meridians // peers
    slopes = jnp.stack([slope_t, slope_q])

    across = [(i, i + 1) for i in range(1, count - 1, 2)]
    across = across + [(b, a) for a, b in across]
    within = [(i, i + 1) for i in range(0, count, 2)]
    within = within + [(b, a) for a, b in within]

    def along_y(r):
        return [(y * SIDE + x, (y + r) % groups * SIDE + x) for y in range(groups) for x in range(SIDE)]

    along_x = [(y * SIDE + x, y * SIDE + 1 - x) for y in range(groups) for x in range(SIDE)]

    far_edge, near_edge, far_sums = edges_call(u, v)
    far_sums = lax.ppermute(far_sums, "space", across)
    far = lax.ppermute(far_edge, "space", across)
    near = lax.ppermute(near_edge, "space", within)

    g_shape = jax.ShapeDtypeStruct((width, width), jnp.float32)
    handed = lambda n: (jax.ShapeDtypeStruct((SIDE, n, chunk, width), jnp.bfloat16),) * groups

    dma = pltpu.SemaphoreType.DMA
    sum_shape = (3 * EDGE, meridians, levels)
    late_shape = jax.ShapeDtypeStruct((peers, EDGE, chunk, width), jnp.bfloat16)
    g, *means = pl.pallas_call(
        functools.partial(early_kernel, chunk),
        name="early_rows",
        out_shape=(g_shape,) + handed(parallels - EDGE),
        in_specs=[ANY] * 5 + [VMEM] * 3,
        out_specs=(VMEM,) + (ANY,) * groups,
        scratch_shapes=row_scratch(dims, parallels - EDGE, parallels + EDGE)
        + [pltpu.VMEM((peers, parallels - EDGE, chunk, width), jnp.bfloat16), dma((6,)), dma((groups,))],
        compiler_params=params(26),
        cost_estimate=row_cost(dims, parallels - EDGE),
    )(u, v, in_hbm(h), in_hbm(q), near, psi, bal, slopes)
    after = means[0]
    means = [x if r == 0 else lax.ppermute(x, "member", along_y(r)) for r, x in enumerate(means)]

    late, *far_means = pl.pallas_call(
        functools.partial(far_means_kernel, chunk),
        name="far_means",
        out_shape=(late_shape,) + handed(EDGE),
        in_specs=[ANY] * 5 + [VMEM] * 4,
        out_specs=(VMEM,) + (ANY,) * groups,
        scratch_shapes=row_scratch(dims, EDGE, 3 * EDGE)[:10]
        + [pltpu.VMEM(sum_shape, jnp.float32)] * 2
        + [dma((4,)), dma((groups,))],
        compiler_params=params(14),
        cost_estimate=row_cost(dims, EDGE),
    )(u, v, h, q, after, far_sums, psi, bal, slopes)
    far_means = [x if r == 0 else lax.ppermute(x, "member", along_y(r)) for r, x in enumerate(far_means)]

    halves = []
    for part in (means, far_means):
        rows = sum(x.shape[1] for x in part[::groups])
        half = jax.ShapeDtypeStruct((rows, chunk, width), jnp.bfloat16)
        g, mine, theirs = pl.pallas_call(
            functools.partial(between_kernel, members),
            name="between",
            out_shape=(g_shape, half, half),
            in_specs=[VMEM] * (1 + len(part)),
            out_specs=(VMEM, VMEM, VMEM),
            compiler_params=params(12),
            cost_estimate=cost(1 << 29, 3 << 20),
        )(g, *part)
        halves += [mine, lax.ppermute(theirs, "member", along_x)]

    g = pl.pallas_call(
        functools.partial(far_kernel, chunk),
        name="far_rows",
        out_shape=g_shape,
        in_specs=[ANY] * 5 + [VMEM] * 5,
        out_specs=VMEM,
        scratch_shapes=row_scratch(dims, EDGE, 3 * EDGE) + [dma((6,))],
        compiler_params=params(16),
        cost_estimate=row_cost(dims, EDGE),
    )(u, v, h, q, far, late, psi, bal, slopes, g)

    g = pl.pallas_call(
        functools.partial(halves_kernel, members * groups / 2.0),
        name="halves",
        out_shape=g_shape,
        in_specs=[VMEM] * (1 + len(halves)),
        out_specs=VMEM,
        compiler_params=params(8),
        cost_estimate=cost(1 << 28, 3 << 20),
    )(g, *halves)

    parts = lax.all_to_all(g.reshape(peers, width // peers, width), "member", 0, 0, tiled=True)
    scale = 1.0 / ((members * peers - 1) * parallels * meridians)
    return (jnp.sum(parts, axis=0) * scale)[None]


def solution(mesh):
    placed = (P("member", "space", None, None),) * 4 + (P("space", None),) * 2 + (P(), P())
    return jax.shard_map(
        on_device, mesh=mesh, in_specs=placed, out_specs=P("space", "member", None), check_vma=False
    )
```

```python
import functools

import jax
import jax.numpy as jnp
from jax import lax
from jax.experimental import pallas as pl
from jax.experimental.pallas import tpu as pltpu
from jax.sharding import PartitionSpec as P

ANY = pl.BlockSpec(memory_space=pl.ANY)
VMEM = pl.BlockSpec(memory_space=pltpu.VMEM)
SIDE = 2
EDGE = 2


def params(mebibytes):
    return pltpu.CompilerParams(vmem_limit_bytes=mebibytes << 20)


def in_hbm(x):
    return pltpu.with_memory_space_constraint(x, pltpu.HBM)


def cost(flops, moved):
    return pl.CostEstimate(flops=flops, bytes_accessed=moved, transcendentals=0)


def gram(a, b):
    return lax.dot_general(a, b, (((0,), (0,)), ((), ())), preferred_element_type=jnp.float32)


def core_index():
    return lax.axis_index("space") % 2


def run(copies):
    for copy in copies:
        copy.start()


def finish(copies):
    for copy in copies:
        copy.wait()


def edges_kernel(u_hbm, v_hbm, far_ref, near_ref, sums_ref, sems):
    parallels = u_hbm.shape[1]
    core = core_index()
    winds = tuple(enumerate((u_hbm, v_hbm)))
    far_at = pl.ds((parallels - EDGE) * core, EDGE)
    near_at = pl.ds((parallels - EDGE) * (1 - core), EDGE)
    far = [pltpu.make_async_copy(x.at[:, far_at], far_ref.at[f], sems.at[f]) for f, x in winds]
    near = [pltpu.make_async_copy(x.at[:, near_at], near_ref.at[f], sems.at[2 + f]) for f, x in winds]
    run(far + near)
    for f, copy in enumerate(far):
        copy.wait()
        for r in range(EDGE):
            total = far_ref[f, 0, r].astype(jnp.float32)
            for m in range(1, far_ref.shape[1]):
                total = total + far_ref[f, m, r].astype(jnp.float32)
            sums_ref[f, r] = total.astype(jnp.bfloat16)
    finish(near)


def edges_call(u, v):
    members, _, meridians, levels = u.shape
    edge = jax.ShapeDtypeStruct((2, members, EDGE, meridians, levels), u.dtype)
    return pl.pallas_call(
        edges_kernel,
        name="edges",
        out_shape=(edge, edge, jax.ShapeDtypeStruct((2, EDGE, meridians, levels), u.dtype)),
        in_specs=[ANY, ANY],
        out_specs=(VMEM, VMEM, VMEM),
        scratch_shapes=[pltpu.SemaphoreType.DMA((4,))],
        compiler_params=params(8),
        cost_estimate=cost(1 << 20, 6 << 20),
    )(in_hbm(u), in_hbm(v))


def spread_over(at, psi_ref, bal_ref, slope_t, levels):
    shape = (levels, psi_ref.shape[1])
    psi = jnp.transpose(jnp.broadcast_to(psi_ref[pl.ds(at, 1), :] * (1.0 / 12.0), shape))
    balance = jnp.transpose(jnp.broadcast_to(bal_ref[pl.ds(at, 1), :], shape))
    return psi, balance * slope_t


def lat_diff(rows):
    return (rows[2] - rows[1]) * 8.0 - (rows[3] - rows[0])


def add_gram(g_ref, a):
    half = a.shape[1] // 2
    g_ref[0:half] += gram(a[:, :half], a)
    g_ref[half:, half:] += gram(a[:, half:], a[:, half:])


def compute_rows(n, row_from, winds, scalars, psi_ref, bal_ref, slopes_ref, work, g_ref, m_ref, known, chunk, ready=lambda: None):
    u_ext, v_ext = winds
    h_buf, q_buf = scalars
    d_bufs, psi_bs, sb_bs, s_bufs = work[0:2], work[2:4], work[4:6], work[6:8]
    members, _, meridians, levels = u_ext.shape
    row = lax.broadcasted_iota(jnp.int32, (meridians, meridians), 0)
    col = lax.broadcasted_iota(jnp.int32, (meridians, meridians), 1)
    east = (row + 1) % meridians == col
    west = (row + meridians - 1) % meridians == col
    stencil = jnp.where(east, 6.0, jnp.where(west, -6.0, 0.0)).astype(jnp.bfloat16)
    slope_t = slopes_ref[0:1, :]
    slope_q = slopes_ref[1:2, :]
    half = meridians // 2
    cuts = [slice(f * levels, (f + 1) * levels) for f in range(4)]

    def prepare(k):
        b = k % 2
        psi_bs[b][...], sb_bs[b][...] = spread_over(row_from + k, psi_ref, bal_ref, slope_t, levels)
        for m in range(members):
            both = jnp.concatenate([v_ext[m, k + EDGE], u_ext[m, k + EDGE]], axis=1)
            d_bufs[b][m] = jnp.dot(stencil, both, preferred_element_type=jnp.float32)

    def derive(k, part):
        b = k % 2
        s_buf = s_bufs[part]
        for start in range(0, half, chunk):
            c = (part * half + start) // chunk
            at = slice(c * chunk, (c + 1) * chunk)
            to = slice(start, start + chunk)
            psi = psi_bs[b][at, :]
            sb = sb_bs[b][at, :]
            total = [None] * 4
            for m in range(members):
                du = lat_diff([u_ext[m, k + e, at, :].astype(jnp.float32) for e in (0, 1, 3, 4)])
                dv = lat_diff([v_ext[m, k + e, at, :].astype(jnp.float32) for e in (0, 1, 3, 4)])
                curl = psi * (d_bufs[b][m, at, 0:levels] - du)
                spread = psi * (d_bufs[b][m, at, levels : 2 * levels] + dv)
                heat = h_buf[m, k, at, :].astype(jnp.float32) - sb * curl
                moist = q_buf[m, k, at, :].astype(jnp.float32) - slope_q * heat
                for f, x in enumerate((curl, spread, heat, moist)):
                    x = x.astype(jnp.bfloat16)
                    if known:
                        mean = m_ref[c, k, :, cuts[f]].astype(jnp.float32)
                        s_buf[m, to, cuts[f]] = (x.astype(jnp.float32) - mean).astype(jnp.bfloat16)
                    else:
                        s_buf[m, to, cuts[f]] = x
                        x = x.astype(jnp.float32)
                        total[f] = x if m == 0 else total[f] + x
            if not known:
                for f, cut in enumerate(cuts):
                    mean = total[f] * (1.0 / members)
                    m_ref[c, k, :, cut] = mean.astype(jnp.bfloat16)
                    for m in range(members):
                        s_buf[m, to, cut] = (s_buf[m, to, cut].astype(jnp.float32) - mean).astype(jnp.bfloat16)

    def take(part):
        s_buf = s_bufs[part]
        add_gram(g_ref, s_buf[...].reshape(-1, s_buf.shape[2]))

    prepare(0)
    ready()
    for k in range(n):
        derive(k, 0)
        if k > 0:
            take(1)
        if k + 1 < n:
            prepare(k + 1)
        derive(k, 1)
        take(0)
    take(1)


def scatter_means(m_scr, outs, first, sem, groups):
    y = lax.axis_index("member") // SIDE
    n = m_scr.shape[1]
    return [
        pltpu.make_async_copy(
            m_scr.at[pl.ds(SIDE * lax.rem(y + r, groups), SIDE)], out.at[:, pl.ds(first, n)], sem.at[r]
        )
        for r, out in enumerate(outs)
    ]


def inner_kernel(chunk, u_hbm, v_hbm, h_hbm, q_hbm, psi_ref, bal_ref, slopes_ref, g_ref, *rest):
    outs, scratch = rest[:-15], rest[-15:]
    u_ext, v_ext, h_buf, q_buf = scratch[:4]
    work = scratch[4:12]
    m_scr, sems, out_sems = scratch[12:]
    n = m_scr.shape[1]
    inner = pl.ds(EDGE, n)
    pairs = ((u_hbm, u_ext), (v_hbm, v_ext), (h_hbm.at[:, inner], h_buf), (q_hbm.at[:, inner], q_buf))
    copies = [pltpu.make_async_copy(x, y, sems.at[i]) for i, (x, y) in enumerate(pairs)]
    run(copies)
    g_ref[...] = jnp.zeros_like(g_ref)
    finish(copies[:2])
    compute_rows(n, EDGE, (u_ext, v_ext), (h_buf, q_buf), psi_ref, bal_ref, slopes_ref, work, g_ref, m_scr, False, chunk, lambda: finish(copies[2:]))
    sends = scatter_means(m_scr, outs, 0, out_sems, len(outs))
    run(sends)
    finish(sends)


def edge_copies(side, u_hbm, v_hbm, h_hbm, q_hbm, halo, u_ext, v_ext, h_buf, q_buf, sems):
    parallels = u_hbm.shape[1]
    own = u_ext.shape[1] - EDGE
    own_from = pl.ds((parallels - own) * side, own)
    own_to = pl.ds(EDGE * (1 - side), own)
    halo_to = pl.ds(own * side, EDGE)
    row_from = pl.ds((parallels - EDGE) * side, EDGE)
    copies = [
        pltpu.make_async_copy(u_hbm.at[:, own_from], u_ext.at[:, own_to], sems.at[0]),
        pltpu.make_async_copy(v_hbm.at[:, own_from], v_ext.at[:, own_to], sems.at[1]),
        pltpu.make_async_copy(h_hbm.at[:, row_from], h_buf, sems.at[2]),
        pltpu.make_async_copy(q_hbm.at[:, row_from], q_buf, sems.at[3]),
    ]
    if halo is not None:
        copies.append(pltpu.make_async_copy(halo.at[0], u_ext.at[:, halo_to], sems.at[4]))
        copies.append(pltpu.make_async_copy(halo.at[1], v_ext.at[:, halo_to], sems.at[5]))
    return copies


def near_kernel(chunk, u_hbm, v_hbm, h_hbm, q_hbm, near_hbm, psi_ref, bal_ref, slopes_ref, g_in_ref, g_ref, *rest):
    outs, scratch = rest[:-15], rest[-15:]
    u_ext, v_ext, h_buf, q_buf = scratch[:4]
    work = scratch[4:12]
    m_scr, sems, out_sems = scratch[12:]
    side = 1 - core_index()
    copies = edge_copies(side, u_hbm, v_hbm, h_hbm, q_hbm, near_hbm, u_ext, v_ext, h_buf, q_buf, sems)
    run(copies)
    g_ref[...] = g_in_ref[...]
    finish(copies)
    row_from = (u_hbm.shape[1] - EDGE) * side
    compute_rows(EDGE, row_from, (u_ext, v_ext), (h_buf, q_buf), psi_ref, bal_ref, slopes_ref, work, g_ref, m_scr, False, chunk)
    sends = scatter_means(m_scr, outs, 0, out_sems, len(outs))
    run(sends)
    finish(sends)


def far_means_kernel(chunk, u_hbm, v_hbm, h_hbm, q_hbm, after_hbm, far_sums_ref, psi_ref, bal_ref, slopes_ref, late_ref, *rest):
    del after_hbm
    outs, scratch = rest[:-14], rest[-14:]
    u_ext, v_ext, h_buf, q_buf = scratch[:4]
    work = scratch[4:10]
    u_sum, v_sum, sems, out_sems = scratch[10:]
    members, parallels, meridians, levels = u_hbm.shape
    copies = edge_copies(core_index(), u_hbm, v_hbm, h_hbm, q_hbm, None, u_ext, v_ext, h_buf, q_buf, sems)
    run(copies)
    finish(copies)
    core = core_index()
    own = 2 * EDGE
    row_from = (parallels - EDGE) * core
    for f, (ext, total) in enumerate(((u_ext, u_sum), (v_ext, v_sum))):
        for r in range(EDGE):
            total[own * core + r] = far_sums_ref[f, r].astype(jnp.float32)
        for r in range(own):
            total[EDGE * (1 - core) + r] = sum(ext[m, EDGE * (1 - core) + r].astype(jnp.float32) for m in range(members))
    for k in range(EDGE):
        work[2][...], work[4][...] = spread_over(row_from + k, psi_ref, bal_ref, slopes_ref[0:1, :], levels)
        for c in range(meridians // chunk):
            at = slice(c * chunk, (c + 1) * chunk)
            du = lat_diff([u_sum[k + e, at] for e in (0, 1, 3, 4)])
            dv = lat_diff([v_sum[k + e, at] for e in (0, 1, 3, 4)])
            work[0][0, at, 0:levels] = du
            work[0][0, at, levels : 2 * levels] = dv
        east = [(pltpu.roll(x[k + EDGE], meridians - 1, 0) - pltpu.roll(x[k + EDGE], 1, 0)) * 6.0 for x in (v_sum, u_sum)]
        work[1][0, :, 0:levels] = east[0]
        work[1][0, :, levels : 2 * levels] = east[1]
        for c in range(meridians // chunk):
            at = slice(c * chunk, (c + 1) * chunk)
            psi = work[2][at]
            curl = psi * (work[1][0, at, 0:levels] - work[0][0, at, 0:levels])
            spread = psi * (work[1][0, at, levels : 2 * levels] + work[0][0, at, levels : 2 * levels])
            heat = sum(h_buf[m, k, at].astype(jnp.float32) for m in range(members)) - work[4][at] * curl
            moist = sum(q_buf[m, k, at].astype(jnp.float32) for m in range(members)) - slopes_ref[1:2, :] * heat
            for f, x in enumerate((curl, spread, heat, moist)):
                late_ref[c, k, :, f * levels : (f + 1) * levels] = (x * (1.0 / members)).astype(jnp.bfloat16)
    sends = scatter_means(late_ref, outs, 0, out_sems, len(outs))
    run(sends)
    finish(sends)


def far_kernel(chunk, u_hbm, v_hbm, h_hbm, q_hbm, far_hbm, late_ref, psi_ref, bal_ref, slopes_ref, g_in_ref, g_ref, *scratch):
    u_ext, v_ext, h_buf, q_buf = scratch[:4]
    work = scratch[4:12]
    sems = scratch[12]
    core = core_index()
    copies = edge_copies(core, u_hbm, v_hbm, h_hbm, q_hbm, far_hbm, u_ext, v_ext, h_buf, q_buf, sems)
    run(copies)
    g_ref[...] = g_in_ref[...]
    finish(copies)
    row_from = (u_hbm.shape[1] - EDGE) * core
    compute_rows(EDGE, row_from, (u_ext, v_ext), (h_buf, q_buf), psi_ref, bal_ref, slopes_ref, work, g_ref, late_ref, True, chunk)


def halves_kernel(weight, g_in_ref, *rest):
    means, g_ref = rest[:-1], rest[-1]
    apart = [x[...].astype(jnp.float32) - y[...].astype(jnp.float32) for x, y in zip(means[::2], means[1::2])]
    apart = jnp.concatenate([x.astype(jnp.bfloat16).reshape(-1, x.shape[2]) for x in apart], axis=0)
    half = g_ref.shape[0] // 2
    top = g_in_ref[0:half] + gram(apart[:, :half], apart) * weight
    g_ref[0:half] = top
    g_ref[half:, 0:half] = jnp.transpose(top[:, half:])
    g_ref[half:, half:] = g_in_ref[half:, half:] + gram(apart[:, half:], apart[:, half:]) * weight


def row_scratch(dims, n, ext):
    members, _, meridians, levels = dims
    return (
        [pltpu.VMEM((members, ext, meridians, levels), jnp.bfloat16)] * 2
        + [pltpu.VMEM((members, n, meridians, levels), jnp.bfloat16)] * 2
        + [pltpu.VMEM((members, meridians, 2 * levels), jnp.float32)] * 2
        + [pltpu.VMEM((meridians, levels), jnp.float32)] * 4
        + [pltpu.VMEM((members, meridians // 2, 4 * levels), jnp.bfloat16)] * 2
    )


def row_cost(dims, n):
    members, _, meridians, levels = dims
    return cost(16 * n * members * meridians * 16 * levels * levels, 32 << 20)


def between_kernel(members, g_in_ref, *rest):
    parts, (g_ref, mine_ref, theirs_ref) = rest[:-3], rest[-3:]
    side = lax.axis_index("member") % SIDE
    groups = lax.axis_size("member") // SIDE
    width = parts[0].shape[3]
    half = width // 2
    low = side == 0
    apart = []
    first = 0
    for at in range(0, len(parts), groups):
        part = parts[at : at + groups]
        n = part[0].shape[1]
        overall = sum(p[...].astype(jnp.float32) for p in part) * (1.0 / groups)
        apart += [(p[...].astype(jnp.float32) - overall).astype(jnp.bfloat16).reshape(-1, width) for p in part]
        overall = overall.astype(jnp.bfloat16)
        mine_ref[first : first + n] = jnp.where(low, overall[0], overall[1])
        theirs_ref[first : first + n] = jnp.where(low, overall[1], overall[0])
        first += n
    apart = jnp.concatenate(apart, axis=0)
    g_ref[0:half] = g_in_ref[0:half] + gram(apart[:, :half], apart) * float(members)
    g_ref[half:, half:] = g_in_ref[half:, half:] + gram(apart[:, half:], apart[:, half:]) * float(members)


def on_device(u, v, h, q, psi, bal, slope_t, slope_q):
    dims = members, parallels, meridians, levels = u.shape
    width = 4 * levels
    count = lax.axis_size("space")
    peers = lax.axis_size("member")
    groups = peers // SIDE
    chunk = meridians // peers
    inner = parallels - 2 * EDGE
    slopes = jnp.stack([slope_t, slope_q])

    across = [(i, i + 1) for i in range(1, count - 1, 2)]
    across = across + [(b, a) for a, b in across]
    within = [(i, i + 1) for i in range(0, count, 2)]
    within = within + [(b, a) for a, b in within]

    def along_y(r):
        return [(y * SIDE + x, (y + r) % groups * SIDE + x) for y in range(groups) for x in range(SIDE)]

    along_x = [(y * SIDE + x, y * SIDE + 1 - x) for y in range(groups) for x in range(SIDE)]

    far_edge, near_edge, far_sums = edges_call(u, v)
    far_sums = lax.ppermute(far_sums, "space", across)
    far = lax.ppermute(far_edge, "space", across)
    near = lax.ppermute(near_edge, "space", within)

    g_shape = jax.ShapeDtypeStruct((width, width), jnp.float32)
    handed = lambda n: (jax.ShapeDtypeStruct((SIDE, n, chunk, width), jnp.bfloat16),) * groups

    dma = pltpu.SemaphoreType.DMA
    sum_shape = (3 * EDGE, meridians, levels)
    late_shape = jax.ShapeDtypeStruct((peers, EDGE, chunk, width), jnp.bfloat16)
    g, *means = pl.pallas_call(
        functools.partial(inner_kernel, chunk),
        name="inner_rows",
        out_shape=(g_shape,) + handed(inner),
        in_specs=[ANY] * 4 + [VMEM] * 3,
        out_specs=(VMEM,) + (ANY,) * groups,
        scratch_shapes=row_scratch(dims, inner, parallels)
        + [pltpu.VMEM((peers, inner, chunk, width), jnp.bfloat16), dma((4,)), dma((groups,))],
        compiler_params=params(22),
        cost_estimate=row_cost(dims, inner),
    )(u, v, in_hbm(h), in_hbm(q), psi, bal, slopes)
    means = [x if r == 0 else lax.ppermute(x, "member", along_y(r)) for r, x in enumerate(means)]

    g, *near_means = pl.pallas_call(
        functools.partial(near_kernel, chunk),
        name="near_rows",
        out_shape=(g_shape,) + handed(EDGE),
        in_specs=[ANY] * 5 + [VMEM] * 4,
        out_specs=(VMEM,) + (ANY,) * groups,
        scratch_shapes=row_scratch(dims, EDGE, 3 * EDGE)
        + [pltpu.VMEM((peers, EDGE, chunk, width), jnp.bfloat16), dma((6,)), dma((groups,))],
        compiler_params=params(16),
        cost_estimate=row_cost(dims, EDGE),
    )(u, v, h, q, near, psi, bal, slopes, g)
    after = near_means[0]
    near_means = [x if r == 0 else lax.ppermute(x, "member", along_y(r)) for r, x in enumerate(near_means)]

    late, *far_means = pl.pallas_call(
        functools.partial(far_means_kernel, chunk),
        name="far_means",
        out_shape=(late_shape,) + handed(EDGE),
        in_specs=[ANY] * 5 + [VMEM] * 4,
        out_specs=(VMEM,) + (ANY,) * groups,
        scratch_shapes=row_scratch(dims, EDGE, 3 * EDGE)[:10]
        + [pltpu.VMEM(sum_shape, jnp.float32)] * 2
        + [dma((4,)), dma((groups,))],
        compiler_params=params(14),
        cost_estimate=row_cost(dims, EDGE),
    )(u, v, h, q, after, far_sums, psi, bal, slopes)
    far_means = [x if r == 0 else lax.ppermute(x, "member", along_y(r)) for r, x in enumerate(far_means)]

    halves = []
    for part in (means + near_means, far_means):
        rows = sum(x.shape[1] for x in part[::groups])
        half = jax.ShapeDtypeStruct((rows, chunk, width), jnp.bfloat16)
        g, mine, theirs = pl.pallas_call(
            functools.partial(between_kernel, members),
            name="between",
            out_shape=(g_shape, half, half),
            in_specs=[VMEM] * (1 + len(part)),
            out_specs=(VMEM, VMEM, VMEM),
            compiler_params=params(12),
            cost_estimate=cost(1 << 29, 3 << 20),
        )(g, *part)
        halves += [mine, lax.ppermute(theirs, "member", along_x)]

    g = pl.pallas_call(
        functools.partial(far_kernel, chunk),
        name="far_rows",
        out_shape=g_shape,
        in_specs=[ANY] * 5 + [VMEM] * 5,
        out_specs=VMEM,
        scratch_shapes=row_scratch(dims, EDGE, 3 * EDGE) + [dma((6,))],
        compiler_params=params(16),
        cost_estimate=row_cost(dims, EDGE),
    )(u, v, h, q, far, late, psi, bal, slopes, g)

    g = pl.pallas_call(
        functools.partial(halves_kernel, members * groups / 2.0),
        name="halves",
        out_shape=g_shape,
        in_specs=[VMEM] * (1 + len(halves)),
        out_specs=VMEM,
        compiler_params=params(8),
        cost_estimate=cost(1 << 28, 3 << 20),
    )(g, *halves)

    parts = lax.all_to_all(g.reshape(peers, width // peers, width), "member", 0, 0, tiled=True)
    scale = 1.0 / ((members * peers - 1) * parallels * meridians)
    return (jnp.sum(parts, axis=0) * scale)[None]


def solution(mesh):
    placed = (P("member", "space", None, None),) * 4 + (P("space", None),) * 2 + (P(), P())
    return jax.shard_map(
        on_device, mesh=mesh, in_specs=placed, out_specs=P("space", "member", None), check_vma=False
    )
```
